128 devices in a mesh: row: 32 (over x, y, core), col: 4 (over z).
Axes of the slice: x: 4, y: 4, z: 4, core: 2. Of those that a mesh axis runs over, the one named last changes fastest.
Arguments:
- kernel: float32 [16384, 16384], P('row', 'col'), may hold values from -7 to 7, as said below
- nugget: float32 [16384], P('row'), may hold values from 0.25 to 1
Outputs:
- factored: float32 [16384, 16384], P('row', 'col')
The draws below stay inside these ranges and needn't reach their ends.
Inputs may be any that keep to these rules, and one draw needn't show every extreme that they name: In matrix order the kernel is symmetric and positive semidefinite.
All inputs are finite; a program needn't handle non-finite values.
Results may differ from the reference program's by a relative error of at most 0.0018.
Values may be sent and summed in bfloat16 or wider, within the bound.
A program may use at most 192 MiB of HBM per device.

```python
import math
import jax
import jax.numpy as jnp
from jax import lax

N = 16384
B = 256
STEPS = 7
DIM = 64
FEAT = 4096
ROWS_DEV = 512
COLS_DEV = 4096


def natural_of_stored_drawn(total_count, per_device, tile_width):
    stored = jnp.arange(total_count, dtype=jnp.int32)
    grid_size = total_count // per_device
    device = stored // per_device
    within = stored % per_device
    return (within // tile_width * grid_size + device) * tile_width + within % tile_width


def draw_kernel(key, part):
    gen_key, dim_key, freq_key = jax.random.split(key, 3)
    generator = jax.random.randint(gen_key, (DIM,), 1, N)
    dim_pick = jax.random.randint(dim_key, (2, FEAT), 0, DIM)
    frequency = jax.random.randint(freq_key, (2, FEAT), 1, 17).astype(jnp.float32)

    def features(natural):
        points = (natural[:, None] * generator[None, :] % N).astype(jnp.float32) / N
        folded = 1.0 - jnp.abs(2.0 * points - 1.0)
        cos_first = jnp.cos(math.pi * frequency[0][None, :] * jnp.take(folded, dim_pick[0], axis=1))
        cos_second = jnp.cos(math.pi * frequency[1][None, :] * jnp.take(folded, dim_pick[1], axis=1))
        return cos_first * cos_second
    row_features = features(natural_of_stored_drawn(N, ROWS_DEV, B))
    col_features = features(natural_of_stored_drawn(N, COLS_DEV, B))
    return jnp.dot(row_features, col_features.T, precision=lax.Precision.HIGHEST) * (4.0 / FEAT)


def steps_of(key, shape, cuts, low, largest):
    loudness, own = 1.0, jax.random.fold_in(key, 6)
    for axis_at, parts in cuts:
        heights = jnp.exp(jax.random.uniform(jax.random.fold_in(own, axis_at), (parts,), jnp.float32, low / len(cuts), largest / len(cuts)))
        loudness = loudness * jnp.repeat(heights, shape[axis_at] // parts).reshape([-1 if axis == axis_at else 1 for axis in range(len(shape))])
    return loudness


def setup_inputs(seed: int = 0) -> dict:
    streams_of = jax.random.split(jax.random.key(seed), 3)
    kernel = draw_kernel(jax.random.fold_in(streams_of[2], 71), 0)
    nugget = jnp.clip(jnp.exp(math.log(1.0) - 1.3862944 * jax.random.uniform(streams_of[1], (N,), jnp.float32) ** steps_of(streams_of[1], (N,), ((0, 32),), -0.2, 0.2)), 0.25, 1.0)
    return {"kernel": kernel, "nugget": nugget}


def stored_of_natural(total_count, per_device, tile_width):
    natural = jnp.arange(total_count, dtype=jnp.int32)
    grid_size = total_count // per_device
    tile_index = natural // tile_width
    return tile_index % grid_size * per_device + tile_index // grid_size * tile_width + natural % tile_width

def natural_of_stored(total_count, per_device, tile_width):
    stored = jnp.arange(total_count, dtype=jnp.int32)
    grid_size = total_count // per_device
    device = stored // per_device
    within = stored % per_device
    return (within // tile_width * grid_size + device) * tile_width + within % tile_width

def reference(kernel, nugget):
    from_rows = stored_of_natural(N, ROWS_DEV, B)
    from_cols = stored_of_natural(N, COLS_DEV, B)
    matrix = jnp.take(jnp.take(kernel, from_rows, axis=0), from_cols, axis=1)
    diagonal_at = jnp.arange(N, dtype=jnp.int32)
    matrix = matrix.at[diagonal_at, diagonal_at].add(jnp.take(nugget, from_rows))
    for panel_step in range(STEPS):
        low_edge = panel_step * B
        high_edge = low_edge + B
        factor = jnp.linalg.cholesky(matrix[low_edge:high_edge, low_edge:high_edge])
        solved = lax.linalg.triangular_solve(factor, matrix[high_edge:, low_edge:high_edge], left_side=False, lower=True, transpose_a=True)
        rounded = solved.astype(jnp.bfloat16)
        product = jnp.dot(rounded.astype(jnp.float32), rounded.T.astype(jnp.float32), preferred_element_type=jnp.float32)
        matrix = matrix.at[high_edge:, high_edge:].add(-product)
        matrix = matrix.at[low_edge:high_edge, low_edge:high_edge].set(factor)
        matrix = matrix.at[high_edge:, low_edge:high_edge].set(solved)
        matrix = matrix.at[low_edge:high_edge, high_edge:].set(jnp.float32(0.0))
    to_rows = natural_of_stored(N, ROWS_DEV, B)
    to_cols = natural_of_stored(N, COLS_DEV, B)
    return jnp.take(jnp.take(matrix, to_rows, axis=0), to_cols, axis=1)
```

```python
import jax
import jax.numpy as jnp
from jax import lax
from jax.experimental import pallas as pl
from jax.experimental.pallas import tpu as pltpu
from jax.sharding import PartitionSpec as P

B = 256
H = 128
STEPS = 7
F32 = jnp.float32
BF16 = jnp.bfloat16
MESH = pl.DeviceIdType.MESH
NT = (((1,), (1,)), ((), ()))
NN = (((1,), (0,)), ((), ()))


def dot_full(a, b, dims):
    return lax.dot_general(a, b, dims, precision=lax.Precision.HIGHEST, preferred_element_type=F32)


def dot_bf(a, b, dims):
    return lax.dot_general(a, b, dims, preferred_element_type=F32)


def lane_splat(x, at):
    return jnp.broadcast_to(x[:, at : at + 1], x.shape)


def row_splat(x, at):
    return jnp.broadcast_to(x[at : at + 1, :], x.shape)


def inverse_factor(groups):
    lane = lax.broadcasted_iota(jnp.int32, (8, H), 1)
    sub = lax.broadcasted_iota(jnp.int32, (8, H), 0)
    groups = list(groups)
    result = []
    for b in range(16):
        start = 8 * b
        block = (lane >= start) & (lane < start + 8)
        here = groups[b]
        cols = [lane_splat(here, start + s) for s in range(8)]
        swept = jnp.where(block, jnp.where(lane - start == sub, 1.0, 0.0), here)
        scaled = jnp.zeros((8, H), F32)
        for r in range(8):
            pivot = row_splat(cols[r], r)
            inv = 1.0 / pivot
            row = row_splat(swept, r)
            at_r = sub == r
            scaled = jnp.where(at_r, row * lax.rsqrt(pivot), scaled)
            row = row * inv
            swept = jnp.where(at_r, row, swept - cols[r] * row)
            for j in range(r + 1, 8):
                entry = row_splat(cols[j], r) * inv
                cols[j] = jnp.where(at_r, entry, cols[j] - cols[r] * entry)
        result.append(jnp.where(lane <= sub + start, scaled, 0.0))
        rows = [row_splat(swept, s) for s in range(8)]
        for g in range(b + 1, 16):
            terms = [lane_splat(groups[g], start + s) * rows[s] for s in range(8)]
            while len(terms) > 1:
                terms = [terms[i] + terms[i + 1] for i in range(0, len(terms), 2)]
            groups[g] = jnp.where(block, 0.0, groups[g]) - terms[0]
    return result


def chain_kernel(lead_ref, lead_bf_ref, inv_ref, tiles, diag, inv_half, low, mixed):
    for t in range(28):
        x, y, c = t // 8, t // 2 % 4, t % 2
        tiles[t] = lead_ref[0, x, y] if c == 0 else lead_ref[1, y, x]

    def step(k, carry):
        at = k * (k + 1) // 2 + k

        def half(h, carry):
            @pl.when(h == 0)
            def _():
                diag[...] = tiles[at, 0:H, 0:H]

            done = inverse_factor([diag[8 * g : 8 * g + 8, :] for g in range(16)])
            for g in range(16):
                inv_half[8 * g : 8 * g + 8, :] = done[g]

            @pl.when(h == 0)
            def _():
                first = inv_half[...]
                l21 = dot_full(tiles[at, H:B, 0:H], first, NT)
                diag[...] = tiles[at, H:B, H:B] - dot_full(l21, l21, NT)
                mixed[...] = dot_full(l21, first, NN)
                inv_ref[k, 0:H, 0:H] = first
                inv_ref[k, 0:H, H:B] = jnp.zeros((H, H), F32)

            @pl.when(h == 1)
            def _():
                second = inv_half[...]
                inv_ref[k, H:B, 0:H] = -dot_full(second, mixed[...], NN)
                inv_ref[k, H:B, H:B] = second

            return carry

        lax.fori_loop(0, 2, half, 0)

        def solve(i, carry):
            t = i * (i + 1) // 2 + k
            lead_bf_ref[t] = dot_full(tiles[t], inv_ref[k], NT).astype(BF16)
            return carry

        lax.fori_loop(k + 1, STEPS, solve, 0)

        def update_row(i, carry):
            left = lead_bf_ref[i * (i + 1) // 2 + k]

            def update(j, carry):
                t = i * (i + 1) // 2 + j
                tiles[t] = tiles[t] - dot_bf(left, lead_bf_ref[j * (j + 1) // 2 + k], NT)
                return carry

            return lax.fori_loop(k + 1, i + 1, update, carry)

        return lax.fori_loop(k + 1, STEPS, update_row, carry)

    lax.fori_loop(0, STEPS, step, 0)


def chain(lead):
    vmem = pl.BlockSpec(memory_space=pltpu.VMEM)
    return pl.pallas_call(
        chain_kernel,
        out_shape=(
            jax.ShapeDtypeStruct((28, B, B), BF16),
            jax.ShapeDtypeStruct((STEPS, B, B), F32),
        ),
        in_specs=[vmem],
        out_specs=(vmem, vmem),
        scratch_shapes=[
            pltpu.VMEM((28, B, B), F32),
            pltpu.VMEM((H, H), F32),
            pltpu.VMEM((H, H), F32),
            pltpu.VMEM((H, H), F32),
            pltpu.VMEM((H, H), F32),
        ],
        compiler_params=pltpu.CompilerParams(vmem_limit_bytes=56 * 2**20),
    )(lead)


def place(row):
    core, y, x = row % 2, row // 2 % 4, row // 8
    return core, x * (1 - core) + y * core, y * (1 - core) + x * core


def row_of(core, major, minor):
    x = major * (1 - core) + minor * core
    y = minor * (1 - core) + major * core
    return (x * 4 + y) * 2 + core


def walk_plane(out_ref, send, recv):
    row, col = lax.axis_index("row"), lax.axis_index("col")
    core, major, minor = place(row)

    def copy(ref, to_core, to_major, to_minor, slot):
        return pltpu.make_async_remote_copy(
            src_ref=ref,
            dst_ref=ref,
            send_sem=send.at[slot],
            recv_sem=recv.at[slot],
            device_id=(row_of(to_core, to_major, to_minor), col),
            device_id_type=MESH,
        )

    def ring(block, half_low, half_high, me, device, base):
        after, before = (me + 1) % 4, (me + 3) % 4
        own_up = copy(block(me), *device(after), base)
        own_down = copy(block(me), *device(before), base + 1)
        own_up.start()
        own_down.start()
        own_up.wait_recv()
        far_up = copy(half_low(before), *device(after), base + 2)
        far_up.start()
        own_down.wait_recv()
        far_down = copy(half_high(after), *device(before), base + 3)
        far_down.start()
        return [own_up, own_down, far_up, far_down]

    half = out_ref.shape[3] // 2
    first = ring(
        lambda at: out_ref.at[core, major, at],
        lambda at: out_ref.at[core, major, at, pl.ds(0, half)],
        lambda at: out_ref.at[core, major, at, pl.ds(half, half)],
        minor,
        lambda at: (core, major, at),
        0,
    )
    for entry in first[2:]:
        entry.wait_recv()
    for entry in first:
        entry.wait_send()
    other = 1 - core
    sibling = (other, major * 0 + place(row + 1 - 2 * core)[1], place(row + 1 - 2 * core)[2])
    across = [copy(out_ref.at[core, major], *sibling, 8)]
    across[0].start()
    second = ring(
        lambda at: out_ref.at[core, at],
        lambda at: out_ref.at[core, at, pl.ds(0, 2)],
        lambda at: out_ref.at[core, at, pl.ds(2, 2)],
        major,
        lambda at: (core, at, minor),
        4,
    )
    for step, at in ((9, (major + 3) % 4), (10, (major + 1) % 4)):
        entry = copy(out_ref.at[core, at], *sibling, step)
        entry.start()
        across.append(entry)
    for entry in second[2:]:
        entry.wait_recv()
    entry = copy(out_ref.at[core, (major + 2) % 4], *sibling, 11)
    entry.start()
    across.append(entry)
    for entry in across:
        entry.wait_recv()
    for entry in second + across:
        entry.wait_send()


def lead_kernel(strip_ref, out_ref, fill_send, fill_recv, own_sem, send, recv):
    row, col = lax.axis_index("row"), lax.axis_index("col")
    core, major, minor = place(row)
    is_own = (row >= 28) | ((col == 0) & (row < 2))

    def fill(u, plane, to):
        to_core, to_major, to_minor = place(to)
        return pltpu.make_async_remote_copy(
            src_ref=strip_ref.at[u, pl.ds(0, B)],
            dst_ref=out_ref.at[to_core, to_major, to_minor],
            send_sem=fill_send.at[u, plane],
            recv_sem=fill_recv,
            device_id=(to, plane),
            device_id_type=MESH,
        )

    cases = []
    for u in range(2):
        to = row * (row + 1) // 2 + col + 4 * u
        for plane in range(4):
            cases.append((u, plane, to, (row < STEPS) & (col + 4 * u <= row) & ((to != row) | (col != plane))))
    for u, plane, to, active in cases:
        @pl.when(active)
        def _(u=u, plane=plane, to=to):
            fill(u, plane, to).start()

    @pl.when(is_own)
    def _():
        own = pltpu.make_async_copy(strip_ref.at[0, pl.ds(0, B)], out_ref.at[core, major, minor], own_sem)
        own.start()
        own.wait()

    @pl.when(jnp.logical_not(is_own))
    def _():
        fill(0, 0, row).wait_recv()

    walk_plane(out_ref, send, recv)
    for u, plane, to, active in cases:
        @pl.when(active)
        def _(u=u, plane=plane, to=to):
            fill(u, plane, to).wait_send()


def side_kernel(rows_ref, out_ref, fill_send, fill_recv, own_sem, send, recv):
    row, col = lax.axis_index("row"), lax.axis_index("col")
    core, major, minor = place(row)
    share = rows_ref.shape[0] // 4
    is_source = row % 4 == col

    def fill(e):
        to = row // 4 * 4 + e
        to_core, to_major, to_minor = place(to)
        return pltpu.make_async_remote_copy(
            src_ref=rows_ref.at[pl.ds(e * share, share)],
            dst_ref=out_ref.at[to_core, to_major, to_minor],
            send_sem=fill_send.at[e],
            recv_sem=fill_recv,
            device_id=(to, col),
            device_id_type=MESH,
        )

    for e in range(4):
        @pl.when(is_source & (col != e))
        def _(e=e):
            fill(e).start()

    @pl.when(is_source)
    def _():
        own = pltpu.make_async_copy(
            rows_ref.at[pl.ds(col * share, share)], out_ref.at[core, major, minor], own_sem
        )
        own.start()
        own.wait()

    @pl.when(jnp.logical_not(is_source))
    def _():
        fill(0).wait_recv()

    walk_plane(out_ref, send, recv)
    for e in range(4):
        @pl.when(is_source & (col != e))
        def _(e=e):
            fill(e).wait_send()


def spread(kernel, operand, block, dtype, fills):
    any_space = pl.BlockSpec(memory_space=pl.ANY)
    return pl.pallas_call(
        kernel,
        out_shape=jax.ShapeDtypeStruct((2, 4, 4) + block, dtype),
        in_specs=[any_space],
        out_specs=any_space,
        scratch_shapes=[
            pltpu.SemaphoreType.DMA(fills),
            pltpu.SemaphoreType.DMA,
            pltpu.SemaphoreType.DMA,
            pltpu.SemaphoreType.DMA((12,)),
            pltpu.SemaphoreType.DMA((12,)),
        ],
        compiler_params=pltpu.CompilerParams(has_side_effects=True),
    )(operand)


def rows_kernel(strips_ref, lead_ref, inv_ref, panel_ref, rounded_ref, acc):
    tile, col = lax.axis_index("row"), lax.axis_index("col")
    at_row = lax.broadcasted_iota(jnp.int32, (2 * B, B), 0)
    at_col = lax.broadcasted_iota(jnp.int32, (2 * B, B), 1)

    def step(k, carry):
        acc[...] = strips_ref[k % 4, k // 4]

        def update(j, carry):
            left = rounded_ref[:, pl.ds(pl.multiple_of(j * B, B), B)]
            acc[...] -= dot_bf(left, lead_ref[k * (k + 1) // 2 + j], NT)
            return carry

        lax.fori_loop(0, k, update, 0)
        solved = dot_full(acc[...], inv_ref[k], NT)
        later = (at_row >= B) | (k < tile)
        rounded_ref[:, pl.ds(pl.multiple_of(k * B, B), B)] = jnp.where(later, solved, 0.0).astype(BF16)

        @pl.when(k % 4 == col)
        def _():
            kept = later | ((k == tile) & (at_col <= at_row))
            panel_ref[k // 4] = jnp.where(kept, solved, 0.0)

        return carry

    lax.fori_loop(0, STEPS, step, 0)


def solve_rows(strips, lead, inv):
    vmem = pl.BlockSpec(memory_space=pltpu.VMEM)
    return pl.pallas_call(
        rows_kernel,
        out_shape=(
            jax.ShapeDtypeStruct((2, 2 * B, B), F32),
            jax.ShapeDtypeStruct((2 * B, STEPS * B), BF16),
        ),
        in_specs=[vmem] * 3,
        out_specs=(vmem, vmem),
        scratch_shapes=[pltpu.VMEM((2 * B, B), F32)],
        compiler_params=pltpu.CompilerParams(vmem_limit_bytes=48 * 2**20),
    )(strips, lead, inv)


def trailing_kernel(matrix_ref, nugget_ref, panel_ref, rounded_ref, even_ref, odd_ref, out_ref):
    slot = pl.program_id(0)
    tile, col = lax.axis_index("row"), lax.axis_index("col")
    col_tile = slot * 4 + col

    @pl.when(col_tile < STEPS)
    def _():
        out_ref[...] = panel_ref[0]

    @pl.when(col_tile >= STEPS)
    def _():
        side = jnp.concatenate([even_ref[0, 0, 0], odd_ref[0, 0, 0]], axis=0)
        for s in range(2):
            rows = pl.ds(s * B, B)
            product = dot_bf(rounded_ref[rows, :], side, NT)
            out_ref[rows, :] = matrix_ref[rows, :] - product

            @pl.when(col_tile == s * 32 + tile)
            def _(s=s, rows=rows):
                at_row = lax.broadcasted_iota(jnp.int32, (B, B), 0)
                at_col = lax.broadcasted_iota(jnp.int32, (B, B), 1)
                out_ref[rows, :] += jnp.where(at_row == at_col, nugget_ref[s : s + 1, :], 0.0)

        @pl.when(tile < STEPS)
        def _():
            out_ref[0:B, :] = jnp.zeros((B, B), F32)


def trailing(matrix, nugget, panel, rounded, side):
    rows, cols = matrix.shape
    depth = rounded.shape[1]

    def even(t):
        return (0, t % 8 // 2, 2 * (t % 2) + t // 8, 0, 0)

    def odd(t):
        return (1, 2 * (t % 2) + t // 8, t % 8 // 2, 0, 0)

    return pl.pallas_call(
        trailing_kernel,
        grid=(cols // B,),
        out_shape=jax.ShapeDtypeStruct(matrix.shape, F32),
        in_specs=[
            pl.BlockSpec((rows, B), lambda t: (0, t)),
            pl.BlockSpec((2, B), lambda t: (0, 0)),
            pl.BlockSpec((1, rows, B), lambda t: (jnp.minimum(t, 1), 0, 0)),
            pl.BlockSpec((rows, depth), lambda t: (0, 0)),
            pl.BlockSpec((1, 1, 1, H, depth), even),
            pl.BlockSpec((1, 1, 1, H, depth), odd),
        ],
        out_specs=pl.BlockSpec((rows, B), lambda t: (0, t)),
        compiler_params=pltpu.CompilerParams(vmem_limit_bytes=48 * 2**20),
    )(matrix, nugget, panel, rounded, side, side)


def body(kernel, nugget):
    rows_here = kernel.shape[0]
    tile, col = lax.axis_index("row"), lax.axis_index("col")
    nugget = nugget.reshape(2, B)
    strip = kernel[:, : 2 * B].reshape(rows_here, 2, B).transpose(1, 0, 2)
    col_tile = jnp.arange(2)[:, None, None] * 4 + col
    same = (
        (col_tile == tile)
        & (jnp.arange(rows_here)[None, :, None] == jnp.arange(B)[None, None, :])
    )
    strip = strip + jnp.where(same, nugget[0][None, None, :], 0.0)
    strips = lax.all_gather(strip, "col")
    lead = spread(lead_kernel, strip, (B, B), F32, (2, 4))
    lead_bf, inv = chain(lead)
    panel, rounded = solve_rows(strips, lead_bf, inv)
    side = spread(side_kernel, rounded, (H, STEPS * B), BF16, (4,))
    return trailing(kernel, nugget, panel, rounded, side)


def solution(mesh):
    return jax.shard_map(
        body,
        mesh=mesh,
        in_specs=(P("row", "col"), P("row")),
        out_specs=P("row", "col"),
        check_vma=False,
    )
```

```python
import jax
import jax.numpy as jnp
from jax import lax
from jax.experimental import pallas as pl
from jax.experimental.pallas import tpu as pltpu
from jax.sharding import PartitionSpec as P

B = 256
H = 128
STEPS = 7
F32 = jnp.float32
BF16 = jnp.bfloat16
MESH = pl.DeviceIdType.MESH
NT = (((1,), (1,)), ((), ()))
NN = (((1,), (0,)), ((), ()))


def dot_full(a, b, dims):
    return lax.dot_general(a, b, dims, precision=lax.Precision.HIGHEST, preferred_element_type=F32)


def dot_bf(a, b, dims):
    return lax.dot_general(a, b, dims, preferred_element_type=F32)


def lane_splat(x, at):
    return jnp.broadcast_to(x[:, at : at + 1], x.shape)


def row_splat(x, at):
    return jnp.broadcast_to(x[at : at + 1, :], x.shape)


def inverse_factor(groups, hooks):
    lane = lax.broadcasted_iota(jnp.int32, (8, H), 1)
    sub = lax.broadcasted_iota(jnp.int32, (8, H), 0)
    groups = list(groups)
    result = []
    for b in range(16):
        if b in hooks:
            hooks[b]()
        start = 8 * b
        block = (lane >= start) & (lane < start + 8)
        here = groups[b]
        cols = [lane_splat(here, start + s) for s in range(8)]
        swept = jnp.where(block, jnp.where(lane - start == sub, 1.0, 0.0), here)
        scaled = jnp.zeros((8, H), F32)
        for r in range(8):
            pivot = row_splat(cols[r], r)
            inv = 1.0 / pivot
            row = row_splat(swept, r)
            at_r = sub == r
            scaled = jnp.where(at_r, row * lax.rsqrt(pivot), scaled)
            row = row * inv
            swept = jnp.where(at_r, row, swept - cols[r] * row)
            for j in range(r + 1, 8):
                entry = row_splat(cols[j], r) * inv
                cols[j] = jnp.where(at_r, entry, cols[j] - cols[r] * entry)
        result.append(jnp.where(lane <= sub + start, scaled, 0.0))
        rows = [row_splat(swept, s) for s in range(8)]
        for g in range(b + 1, 16):
            terms = [lane_splat(groups[g], start + s) * rows[s] for s in range(8)]
            while len(terms) > 1:
                terms = [terms[i] + terms[i + 1] for i in range(0, len(terms), 2)]
            groups[g] = jnp.where(block, 0.0, groups[g]) - terms[0]
    return result


def place(row):
    core, y, x = row % 2, row // 2 % 4, row // 8
    return core, x * (1 - core) + y * core, y * (1 - core) + x * core


def row_of(core, major, minor):
    x = major * (1 - core) + minor * core
    y = minor * (1 - core) + major * core
    return (x * 4 + y) * 2 + core


def walk_partners():
    row, col = lax.axis_index("row"), lax.axis_index("col")
    core, major, minor = place(row)
    near = [(core, major, (minor + d) % 4) for d in (1, 3)] + [(core, (major + d) % 4, minor) for d in (1, 3)]
    return [(row_of(*entry), col) for entry in near] + [(row + 1 - 2 * core, col)]


class Walk:
    def __init__(self, low1, high1, low2, high2, whole, send, recv):
        self.row, self.col = lax.axis_index("row"), lax.axis_index("col")
        self.core, self.major, self.minor = place(self.row)
        self.parts = low1, high1, low2, high2, whole
        self.send, self.recv = send, recv

    def copies(self, n):
        low1, high1, low2, high2, whole = self.parts
        core, major, minor = self.core, self.major, self.minor

        def copy(ref, device, slot):
            return lambda: pltpu.make_async_remote_copy(
                src_ref=ref,
                dst_ref=ref,
                send_sem=self.send.at[n, slot],
                recv_sem=self.recv.at[n, slot],
                device_id=(device, self.col),
                device_id_type=MESH,
            )

        def ring(low, high, me, device, base):
            after, before = (me + 1) % 4, (me + 3) % 4
            up, down = device(after), device(before)
            return [
                copy(low(n, me), up, base),
                copy(high(n, me), down, base + 1),
                copy(high(n, me), up, base + 2),
                copy(low(n, me), down, base + 3),
                copy(low(n, before), up, base + 4),
                copy(high(n, after), down, base + 5),
            ]

        first = ring(low1, high1, minor, lambda at: row_of(core, major, at), 0)
        second = ring(low2, high2, major, lambda at: row_of(core, at, minor), 6)
        sibling = self.row + 1 - 2 * core
        order = (major, (major + 3) % 4, (major + 1) % 4, (major + 2) % 4)
        across = [copy(whole(n, at), sibling, 12 + i) for i, at in enumerate(order)]
        return first + second + across

    def begin(self, n):
        sent = self.copies(n)
        for i in range(4):
            sent[i]().start()

    def middle(self, n):
        sent = self.copies(n)
        sent[0]().wait_recv()
        sent[4]().start()
        sent[1]().wait_recv()
        sent[5]().start()

    def second(self, n):
        sent = self.copies(n)
        for i in range(2, 6):
            sent[i]().wait_recv()
        for i in (6, 7, 8, 9, 12):
            sent[i]().start()

    def third(self, n):
        sent = self.copies(n)
        sent[6]().wait_recv()
        sent[10]().start()
        sent[7]().wait_recv()
        sent[11]().start()
        sent[8]().wait_recv()
        sent[13]().start()
        sent[9]().wait_recv()
        sent[14]().start()

    def fourth(self, n):
        sent = self.copies(n)
        sent[10]().wait_recv()
        sent[11]().wait_recv()
        sent[15]().start()

    def finish(self, n):
        sent = self.copies(n)
        for i in range(12, 16):
            sent[i]().wait_recv()
        for entry in sent:
            entry().wait_send()


def index_of(i, j):
    return i * (i + 1) // 2 + j


def lanes(k):
    return pl.ds(pl.multiple_of(k * B, B), B)


def factor_kernel(
    strip_ref, panel_ref, rounded_ref, side_ref,
    tiles, strips, lead, inverse, diag, inv_half, mixed, acc,
    fill_send, fill_recv, own_sem, keep_sem, share_send, share_recv, share_own,
    strip_send, strip_recv, lead_send, lead_recv, side_send, side_recv,
):
    row, col = lax.axis_index("row"), lax.axis_index("col")
    core, major, minor = place(row)
    tile = row
    base = row // 4 * 4
    is_source = row % 4 == col
    share = rounded_ref.shape[0] // 4
    at_row = lax.broadcasted_iota(jnp.int32, (2 * B, B), 0)
    at_col = lax.broadcasted_iota(jnp.int32, (2 * B, B), 1)

    def when(condition, action):
        pl.when(condition)(action)

    def span(start, size):
        return pl.ds(pl.multiple_of(start, 8), size)

    lead_walk = Walk(
        lambda n, at: tiles.at[pl.ds(4 * n, 4), span(8 * (core * 16 + major * 4 + at), 8), pl.ds(0, H)],
        lambda n, at: tiles.at[pl.ds(4 * n, 4), span(8 * (core * 16 + major * 4 + at), 8), pl.ds(H, H)],
        lambda n, at: tiles.at[pl.ds(4 * n, 4), span(8 * (core * 16 + at * 4), 16)],
        lambda n, at: tiles.at[pl.ds(4 * n, 4), span(8 * (core * 16 + at * 4) + 16, 16)],
        lambda n, at: tiles.at[pl.ds(4 * n, 4), span(8 * (core * 16 + at * 4), 32)],
        lead_send,
        lead_recv,
    )
    half = share // 2
    side_walk = Walk(
        lambda n, at: side_ref.at[core, major, at, pl.ds(0, half), lanes(n)],
        lambda n, at: side_ref.at[core, major, at, pl.ds(half, half), lanes(n)],
        lambda n, at: side_ref.at[core, at, pl.ds(0, 2), :, lanes(n)],
        lambda n, at: side_ref.at[core, at, pl.ds(2, 2), :, lanes(n)],
        lambda n, at: side_ref.at[core, at, :, :, lanes(n)],
        side_send,
        side_recv,
    )

    mine = [(index_of(row, col + 4 * u), (row < STEPS) & (col + 4 * u <= row)) for u in range(2)]

    def fill(u, to, plane):
        to_core, to_major, to_minor = place(to)
        piece = span(8 * (to_core * 16 + to_major * 4 + to_minor), 8)
        return pltpu.make_async_remote_copy(
            src_ref=strip_ref.at[u, piece],
            dst_ref=tiles.at[mine[u][0], piece],
            send_sem=fill_send.at[u, plane * 32 + to],
            recv_sem=fill_recv.at[mine[u][0] // 4],
            device_id=(to, plane),
            device_id_type=MESH,
        )

    def fill_own(u):
        piece = span(8 * (core * 16 + major * 4 + minor), 8)
        return pltpu.make_async_copy(
            strip_ref.at[u, piece], tiles.at[mine[u][0], piece], fill_recv.at[mine[u][0] // 4]
        )

    def each_fill(action):
        def one(d, carry):
            to, plane = d // 4, d % 4
            for u in range(2):
                when((to != row) | (plane != col), lambda u=u: when(mine[u][1], lambda: action(fill(u, to, plane))))
            return carry

        @pl.when(row < STEPS)
        def _():
            lax.fori_loop(0, 128, one, 0)

    def lead_begin(n):
        here = tiles.at[pl.ds(4 * n, 4), span(8 * (core * 16 + major * 4 + minor), 8)]
        pltpu.make_async_remote_copy(
            src_ref=here,
            dst_ref=here,
            send_sem=own_sem,
            recv_sem=fill_recv.at[n],
            device_id=(base + (row + 1) % 4, col),
            device_id_type=MESH,
        ).wait_recv()
        lead_walk.begin(n)

    def strip_copies(u):
        after, before = (col + 1) % 4, (col + 3) % 4

        def copy(src, dst, to, slot):
            return lambda: pltpu.make_async_remote_copy(
                src_ref=src,
                dst_ref=dst,
                send_sem=strip_send.at[u, slot],
                recv_sem=strip_recv.at[u, slot],
                device_id=(row, to),
                device_id_type=MESH,
            )

        low, high = pl.ds(0, B), pl.ds(B, B)
        near = [
            copy(strip_ref.at[u, part], strips.at[col, u, part], to, slot)
            for slot, (part, to) in enumerate(((low, after), (high, before), (high, after), (low, before)))
        ]
        up, down = strips.at[before, u, low], strips.at[after, u, high]
        return near + [copy(up, up, after, 4), copy(down, down, before, 5)]

    def strip_begin(u):
        for entry in strip_copies(u)[:4]:
            entry().start()

    def strip_pass(u):
        sent = strip_copies(u)
        sent[0]().wait_recv()
        sent[4]().start()
        sent[1]().wait_recv()
        sent[5]().start()

    def strip_finish(u):
        sent = strip_copies(u)
        for i in range(2, 6):
            sent[i]().wait_recv()
        for entry in sent:
            entry().wait_send()

    keep = pltpu.make_async_copy(strip_ref, strips.at[col], keep_sem)

    def share_copy(n, e):
        to = base + e
        to_core, to_major, to_minor = place(to)
        return pltpu.make_async_remote_copy(
            src_ref=rounded_ref.at[pl.ds(e * share, share), lanes(n)],
            dst_ref=side_ref.at[to_core, to_major, to_minor, :, lanes(n)],
            send_sem=share_send.at[n, e],
            recv_sem=share_recv.at[n],
            device_id=(to, col),
            device_id_type=MESH,
        )

    def share_keep(n):
        return pltpu.make_async_copy(
            rounded_ref.at[pl.ds(pl.multiple_of(col * share, share), share), lanes(n)],
            side_ref.at[core, major, minor, :, lanes(n)],
            share_own,
        )

    def solve(n):
        acc[...] = strips[n % 4, n // 4]

        def update(j, carry):
            acc[...] -= dot_bf(rounded_ref[:, lanes(j)], lead[index_of(n, j)], NT)
            return carry

        lax.fori_loop(0, n, update, 0)
        solved = dot_full(acc[...], inverse[n], NT)
        later = (at_row >= B) | (n < tile)
        rounded_ref[:, lanes(n)] = jnp.where(later, solved, 0.0).astype(BF16)

        @pl.when(n % 4 == col)
        def _():
            kept = later | ((n == tile) & (at_col <= at_row))
            panel_ref[n // 4] = jnp.where(kept, solved, 0.0)

        for e in range(4):
            when(is_source & (col != e), lambda e=e: share_copy(n, e).start())
        when(is_source, lambda: share_keep(n).start())

    def side_begin(n):
        when(is_source, lambda: share_keep(n).wait())
        when(jnp.logical_not(is_source), lambda: share_copy(n, (row + 1) % 4).wait_recv())
        side_walk.begin(n)

    def side_finish(n):
        side_walk.finish(n)
        for e in range(4):
            when(is_source & (col != e), lambda e=e: share_copy(n, e).wait_send())

    around = (1, 2, 3)
    partners = walk_partners() + [(base + (row + d) % 4, col) for d in around] + [(row, (col + d) % 4) for d in (1, 3)]
    barrier = pltpu.get_barrier_semaphore()
    for device in partners:
        pl.semaphore_signal(barrier, inc=1, device_id=device, device_id_type=MESH)

    def greet(d, carry):
        to, plane = d // 4, d % 4

        @pl.when((plane <= to) & ((to != row) | (plane != col)))
        def _():
            pl.semaphore_signal(barrier, inc=1, device_id=(to, plane), device_id_type=MESH)

        return carry

    lax.fori_loop(0, 4 * STEPS, greet, 0)
    owner = (row < STEPS) & (col <= row)
    pl.semaphore_wait(barrier, len(partners) + 127 * owner.astype(jnp.int32))

    each_fill(lambda entry: entry.start())
    for u in range(2):
        when(mine[u][1], lambda u=u: fill_own(u).start())
    strip_begin(0)
    keep.start()
    lead_begin(0)
    lead_walk.middle(0)
    lead_walk.second(0)
    lead_walk.third(0)
    lead_walk.fourth(0)
    keep.wait()

    def step(k, carry):
        lead_walk.finish(k)
        when(k >= 2, lambda: side_finish(k - 2))
        at = index_of(k, k)

        def row_tile(j, carry):
            here = index_of(k, j)

            def update(i, carry):
                tiles[here] -= dot_bf(lead[index_of(k, i)], lead[index_of(j, i)], NT)
                return carry

            lax.fori_loop(0, j, update, 0)
            found = dot_full(tiles[here], inverse[j], NT).astype(BF16)
            lead[here] = found
            tiles[at] -= dot_bf(found, found, NT)
            return carry

        lax.fori_loop(0, k, row_tile, 0)

        @pl.when(k == 1)
        def _():
            strip_finish(0)

        @pl.when(k == 5)
        def _():
            strip_finish(1)

        when(k >= 1, lambda: solve(k - 1))

        def half_step(h, carry):
            more, past = k < STEPS - 1, k >= 1

            def at_half(value, condition, action):
                pl.when((h == value) & condition)(action)

            def early():
                at_half(0, more, lambda: lead_begin(k + 1))
                at_half(0, past, lambda: side_begin(k - 1))
                at_half(1, more, lambda: lead_walk.third(k + 1))

            def late():
                at_half(0, more, lambda: lead_walk.middle(k + 1))
                at_half(0, past, lambda: side_walk.middle(k - 1))
                at_half(1, more, lambda: lead_walk.fourth(k + 1))
                at_half(1, past, lambda: side_walk.third(k - 1))

            @pl.when(h == 0)
            def _():
                diag[...] = tiles[at, 0:H, 0:H]

            done = inverse_factor([diag[8 * g : 8 * g + 8, :] for g in range(16)], {5: early, 10: late})
            for g in range(16):
                inv_half[8 * g : 8 * g + 8, :] = done[g]

            @pl.when(h == 0)
            def _():
                when(more, lambda: lead_walk.second(k + 1))
                when(past, lambda: side_walk.second(k - 1))
                when(k == 0, lambda: strip_pass(0))
                when(k == 0, lambda: strip_begin(1))
                when(k == 2, lambda: strip_pass(1))
                first = inv_half[...]
                l21 = dot_full(tiles[at, H:B, 0:H], first, NT)
                diag[...] = tiles[at, H:B, H:B] - dot_full(l21, l21, NT)
                mixed[...] = dot_full(l21, first, NN)
                inverse[k, 0:H, 0:H] = first
                inverse[k, 0:H, H:B] = jnp.zeros((H, H), F32)

            @pl.when(h == 1)
            def _():
                second = inv_half[...]
                inverse[k, H:B, 0:H] = -dot_full(second, mixed[...], NN)
                inverse[k, H:B, H:B] = second
                when(past, lambda: side_walk.fourth(k - 1))

            return carry

        return lax.fori_loop(0, 2, half_step, carry)

    lax.fori_loop(0, STEPS, step, 0)
    last = STEPS - 1
    side_finish(last - 1)
    solve(last)
    side_begin(last)
    side_walk.middle(last)
    side_walk.second(last)
    side_walk.third(last)
    side_walk.fourth(last)
    side_finish(last)
    each_fill(lambda entry: entry.wait_send())


def factor(strip):
    vmem = pl.BlockSpec(memory_space=pltpu.VMEM)
    anywhere = pl.BlockSpec(memory_space=pl.ANY)
    dma = pltpu.SemaphoreType.DMA
    return pl.pallas_call(
        factor_kernel,
        out_shape=(
            jax.ShapeDtypeStruct((2, 2 * B, B), F32),
            jax.ShapeDtypeStruct((2 * B, STEPS * B), BF16),
            jax.ShapeDtypeStruct((2, 4, 4, H, STEPS * B), BF16),
        ),
        in_specs=[anywhere],
        out_specs=(vmem, vmem, anywhere),
        scratch_shapes=[
            pltpu.VMEM((28, B, B), F32),
            pltpu.VMEM((4, 2, 2 * B, B), F32),
            pltpu.VMEM((28, B, B), BF16),
            pltpu.VMEM((STEPS, B, B), F32),
            pltpu.VMEM((H, H), F32),
            pltpu.VMEM((H, H), F32),
            pltpu.VMEM((H, H), F32),
            pltpu.VMEM((2 * B, B), F32),
            dma((2, 128)), dma((STEPS,)), dma, dma, dma((STEPS, 4)), dma((STEPS,)), dma,
            dma((2, 6)), dma((2, 6)), dma((STEPS, 16)), dma((STEPS, 16)), dma((STEPS, 16)), dma((STEPS, 16)),
        ],
        compiler_params=pltpu.CompilerParams(
            has_side_effects=True, collective_id=0, vmem_limit_bytes=48 * 2**20
        ),
    )(strip)


def trailing_kernel(matrix_ref, nugget_ref, panel_ref, rounded_ref, even_ref, odd_ref, out_ref):
    slot = pl.program_id(0)
    tile, col = lax.axis_index("row"), lax.axis_index("col")
    col_tile = slot * 4 + col

    @pl.when(col_tile < STEPS)
    def _():
        out_ref[...] = panel_ref[0]

    @pl.when(col_tile >= STEPS)
    def _():
        side = jnp.concatenate([even_ref[0, 0, 0], odd_ref[0, 0, 0]], axis=0)
        out_ref[...] = matrix_ref[...] - dot_bf(rounded_ref[...], side, NT)
        for s in range(2):
            rows = pl.ds(s * B, B)

            @pl.when(col_tile == s * 32 + tile)
            def _(s=s, rows=rows):
                at_row = lax.broadcasted_iota(jnp.int32, (B, B), 0)
                at_col = lax.broadcasted_iota(jnp.int32, (B, B), 1)
                out_ref[rows, :] += jnp.where(at_row == at_col, nugget_ref[s : s + 1, :], 0.0)

        @pl.when(tile < STEPS)
        def _():
            out_ref[0:B, :] = jnp.zeros((B, B), F32)


def trailing(matrix, nugget, panel, rounded, side):
    rows, cols = matrix.shape
    depth = rounded.shape[1]

    def even(t):
        return (0, t % 8 // 2, 2 * (t % 2) + t // 8, 0, 0)

    def odd(t):
        return (1, 2 * (t % 2) + t // 8, t % 8 // 2, 0, 0)

    return pl.pallas_call(
        trailing_kernel,
        grid=(cols // B,),
        out_shape=jax.ShapeDtypeStruct(matrix.shape, F32),
        in_specs=[
            pl.BlockSpec((rows, B), lambda t: (0, t)),
            pl.BlockSpec((2, B), lambda t: (0, 0)),
            pl.BlockSpec((1, rows, B), lambda t: (jnp.minimum(t, 1), 0, 0)),
            pl.BlockSpec((rows, depth), lambda t: (0, 0)),
            pl.BlockSpec((1, 1, 1, H, depth), even),
            pl.BlockSpec((1, 1, 1, H, depth), odd),
        ],
        out_specs=pl.BlockSpec((rows, B), lambda t: (0, t)),
        compiler_params=pltpu.CompilerParams(vmem_limit_bytes=48 * 2**20),
    )(matrix, nugget, panel, rounded, side, side)


def body(kernel, nugget):
    rows_here = kernel.shape[0]
    tile, col = lax.axis_index("row"), lax.axis_index("col")
    nugget = nugget.reshape(2, B)
    strip = kernel[:, : 2 * B].reshape(rows_here, 2, B).transpose(1, 0, 2)
    col_tile = jnp.arange(2)[:, None, None] * 4 + col
    same = (
        (col_tile == tile)
        & (jnp.arange(rows_here)[None, :, None] == jnp.arange(B)[None, None, :])
    )
    strip = strip + jnp.where(same, nugget[0][None, None, :], 0.0)
    panel, rounded, side = factor(strip)
    return trailing(kernel, nugget, panel, rounded, side)


def solution(mesh):
    return jax.shard_map(
        body,
        mesh=mesh,
        in_specs=(P("row", "col"), P("row")),
        out_specs=P("row", "col"),
        check_vma=False,
    )
```

```python
import jax
import jax.numpy as jnp
from jax import lax
from jax.experimental import pallas as pl
from jax.experimental.pallas import tpu as pltpu
from jax.sharding import PartitionSpec as P

B = 256
H = 128
STEPS = 7
F32 = jnp.float32
BF16 = jnp.bfloat16
MESH = pl.DeviceIdType.MESH
NT = (((1,), (1,)), ((), ()))
NN = (((1,), (0,)), ((), ()))


def pieces(x):
    high = x.astype(BF16)
    return high, (x - high.astype(F32)).astype(BF16)


def dot_full(a, b, dims):
    a_high, a_low = pieces(a)
    b_high, b_low = pieces(b)
    a_axis, b_axis = dims[0][0][0], dims[0][1][0]
    return dot_bf(
        jnp.concatenate([a_high, a_high, a_low], axis=a_axis),
        jnp.concatenate([b_high, b_low, b_high], axis=b_axis),
        dims,
    )


def dot_inverse(a, terms):
    high, low = pieces(a)
    return dot_bf(jnp.concatenate([high, high, low], axis=1), terms, NT)


def dot_bf(a, b, dims):
    return lax.dot_general(a, b, dims, preferred_element_type=F32)


def lane_splat(x, at):
    return jnp.broadcast_to(x[:, at : at + 1], x.shape)


def row_splat(x, at):
    return jnp.broadcast_to(x[at : at + 1, :], x.shape)


def inverse_factor(groups, hooks):
    lane = lax.broadcasted_iota(jnp.int32, (8, H), 1)
    sub = lax.broadcasted_iota(jnp.int32, (8, H), 0)
    groups = list(groups)
    result = []
    for b in range(16):
        if b in hooks:
            hooks[b]()
        start = 8 * b
        block = (lane >= start) & (lane < start + 8)
        here = groups[b]
        cols = [lane_splat(here, start + s) for s in range(8)]
        swept = jnp.where(block, jnp.where(lane - start == sub, 1.0, 0.0), here)
        scaled = jnp.zeros((8, H), F32)
        for r in range(8):
            pivot = row_splat(cols[r], r)
            inv = 1.0 / pivot
            row = row_splat(swept, r)
            at_r = sub == r
            scaled = jnp.where(at_r, row * lax.rsqrt(pivot), scaled)
            row = row * inv
            swept = jnp.where(at_r, row, swept - cols[r] * row)
            for j in range(r + 1, 8):
                entry = row_splat(cols[j], r) * inv
                cols[j] = jnp.where(at_r, entry, cols[j] - cols[r] * entry)
        result.append(jnp.where(lane <= sub + start, scaled, 0.0))
        rows = [row_splat(swept, s) for s in range(8)]
        for g in range(b + 1, 16):
            terms = [lane_splat(groups[g], start + s) * rows[s] for s in range(8)]
            while len(terms) > 1:
                terms = [terms[i] + terms[i + 1] for i in range(0, len(terms), 2)]
            groups[g] = jnp.where(block, 0.0, groups[g]) - terms[0]
    return result


def place(row):
    core, y, x = row % 2, row // 2 % 4, row // 8
    return core, x * (1 - core) + y * core, y * (1 - core) + x * core


def row_of(core, major, minor):
    x = major * (1 - core) + minor * core
    y = minor * (1 - core) + major * core
    return (x * 4 + y) * 2 + core


class Walk:
    def __init__(self, single, low, high, whole, send, recv):
        self.row, self.col = lax.axis_index("row"), lax.axis_index("col")
        self.core, self.major, self.minor = place(self.row)
        self.parts = single, low, high, whole
        self.send, self.recv = send, recv

    def copies(self, n):
        single, low, high, whole = self.parts
        core, major, minor = self.core, self.major, self.minor

        def copy(ref, device, slot):
            return lambda: pltpu.make_async_remote_copy(
                src_ref=ref,
                dst_ref=ref,
                send_sem=self.send.at[n, slot],
                recv_sem=self.recv.at[n, slot],
                device_id=(device, self.col),
                device_id_type=MESH,
            )

        first = [
            copy(single(n, minor), row_of(core, major, (minor + d) % 4), i) for i, d in enumerate((1, 3, 2))
        ]
        after, before = (major + 1) % 4, (major + 3) % 4
        up, down = row_of(core, after, minor), row_of(core, before, minor)
        second = [
            copy(low(n, major), up, 3),
            copy(high(n, major), down, 4),
            copy(high(n, major), up, 5),
            copy(low(n, major), down, 6),
            copy(low(n, before), up, 7),
            copy(high(n, after), down, 8),
        ]
        sibling = self.row + 1 - 2 * core
        order = (major, before, after, (major + 2) % 4)
        return first + second + [copy(whole(n, at), sibling, 9 + i) for i, at in enumerate(order)]

    def begin(self, n):
        sent = self.copies(n)
        for i in (2, 0, 1):
            sent[i]().start()

    def second(self, n):
        sent = self.copies(n)
        for i in range(3):
            sent[i]().wait_recv()
        for i in (3, 4, 5, 6, 9):
            sent[i]().start()

    def third(self, n):
        sent = self.copies(n)
        sent[3]().wait_recv()
        sent[7]().start()
        sent[4]().wait_recv()
        sent[8]().start()
        sent[5]().wait_recv()
        sent[10]().start()
        sent[6]().wait_recv()
        sent[11]().start()

    def fourth(self, n):
        sent = self.copies(n)
        sent[7]().wait_recv()
        sent[8]().wait_recv()
        sent[12]().start()

    def finish(self, n):
        sent = self.copies(n)
        for i in range(9, 13):
            sent[i]().wait_recv()
        for entry in sent:
            entry().wait_send()


GROUP_START = (0, 10)
GROUP_SIZE = (10, 18)
FROM_PLANE = ((4, 3, 2, 1), (6, 5, 4, 3))


def from_plane_start(group, plane):
    return GROUP_START[group] + sum(FROM_PLANE[group][:plane])


def tile_at(i, j):
    plane = j % 4
    early = 4 * j - j * (j - 1) // 2 + i - j
    late = 10 + 6 * plane - plane * (plane - 1) // 2 + jnp.where(j < 4, i - 4, 3 + i - j)
    return jnp.where(i < 4, early, late)


def index_of(i, j):
    return i * (i + 1) // 2 + j


def lanes(k):
    return pl.ds(pl.multiple_of(k * B, B), B)


def factor_kernel(
    strip_ref, panel_ref, rounded_ref, side_ref,
    tiles, strips, lead, inverse, diag, inv_half, mixed, acc,
    fill_send, fill_recv, onward_send, onward_recv, keep_sem, share_send, share_recv, share_own,
    strip_send, strip_recv, lead_send, lead_recv, side_send, side_recv,
):
    row, col = lax.axis_index("row"), lax.axis_index("col")
    core, major, minor = place(row)
    tile = row
    base = row // 4 * 4
    is_source = row % 4 == col
    share = rounded_ref.shape[0] // 4
    at_row = lax.broadcasted_iota(jnp.int32, (2 * B, B), 0)
    at_col = lax.broadcasted_iota(jnp.int32, (2 * B, B), 1)

    def when(condition, action):
        @pl.when(condition)
        def _():
            action()

    def span(start, size):
        return pl.ds(pl.multiple_of(start, 8), size)

    def group_tiles(g):
        return pl.ds(GROUP_START[g], GROUP_SIZE[g])

    lead_walk = Walk(
        lambda g, at: tiles.at[group_tiles(g), span(8 * (core * 16 + major * 4 + at), 8)],
        lambda g, at: tiles.at[group_tiles(g), span(8 * (core * 16 + at * 4), 16)],
        lambda g, at: tiles.at[group_tiles(g), span(8 * (core * 16 + at * 4) + 16, 16)],
        lambda g, at: tiles.at[group_tiles(g), span(8 * (core * 16 + at * 4), 32)],
        lead_send,
        lead_recv,
    )
    half = 2
    side_walk = Walk(
        lambda n, at: side_ref.at[core, major, at, :, lanes(n)],
        lambda n, at: side_ref.at[core, at, pl.ds(0, half), :, lanes(n)],
        lambda n, at: side_ref.at[core, at, pl.ds(half, half), :, lanes(n)],
        lambda n, at: side_ref.at[core, at, :, :, lanes(n)],
        side_send,
        side_recv,
    )

    piece = span(8 * (core * 16 + major * 4 + minor), 8)
    mine = []
    for u in range(2):
        mine.append((tile_at(row, col + 4 * u), (row >= 4).astype(jnp.int32), (row < STEPS) & (col + 4 * u <= row)))

    def fill(u, to):
        to_core, to_major, to_minor = place(to)
        there = span(8 * (to_core * 16 + to_major * 4 + to_minor), 8)
        return pltpu.make_async_remote_copy(
            src_ref=strip_ref.at[u, there],
            dst_ref=tiles.at[mine[u][0], there],
            send_sem=fill_send.at[u, to],
            recv_sem=fill_recv.at[mine[u][1]],
            device_id=(to, col),
            device_id_type=MESH,
        )

    def fill_own(u):
        return pltpu.make_async_copy(
            strip_ref.at[u, piece], tiles.at[mine[u][0], piece], fill_recv.at[mine[u][1]]
        )

    def each_fill(action):
        def one(to, carry):
            for u in range(2):
                when((to != row) & mine[u][2], lambda u=u: action(fill(u, to)))
            return carry

        when(row < STEPS, lambda: lax.fori_loop(0, 32, one, 0))

    def onward(g, plane, to):
        block = tiles.at[pl.ds(from_plane_start(g, plane), FROM_PLANE[g][plane]), piece]
        return pltpu.make_async_remote_copy(
            src_ref=block,
            dst_ref=block,
            send_sem=onward_send.at[g, to],
            recv_sem=onward_recv.at[g, plane],
            device_id=(row, to),
            device_id_type=MESH,
        )

    def onward_begin(g):
        for plane in range(4):
            @pl.when(col == plane)
            def _(plane=plane):
                block = tiles.at[pl.ds(from_plane_start(g, plane), FROM_PLANE[g][plane]), piece]
                pltpu.make_async_remote_copy(
                    src_ref=block,
                    dst_ref=block,
                    send_sem=onward_send.at[g, plane],
                    recv_sem=fill_recv.at[g],
                    device_id=(base + (row + 1) % 4, col),
                    device_id_type=MESH,
                ).wait_recv()
                for to in range(4):
                    if to != plane:
                        onward(g, plane, to).start()

    def lead_begin(g):
        for plane in range(4):
            when(col != plane, lambda plane=plane: onward(g, plane, (plane + 1) % 4).wait_recv())
        lead_walk.begin(g)

    def onward_finish(g):
        for plane in range(4):
            @pl.when(col == plane)
            def _(plane=plane):
                for to in range(4):
                    if to != plane:
                        onward(g, plane, to).wait_send()

    def strip_copies(u):
        after, before = (col + 1) % 4, (col + 3) % 4

        def copy(src, dst, to, slot):
            return lambda: pltpu.make_async_remote_copy(
                src_ref=src,
                dst_ref=dst,
                send_sem=strip_send.at[u, slot],
                recv_sem=strip_recv.at[u, slot],
                device_id=(row, to),
                device_id_type=MESH,
            )

        low, high = pl.ds(0, B), pl.ds(B, B)
        near = [
            copy(strip_ref.at[u, part], strips.at[col, u, part], to, slot)
            for slot, (part, to) in enumerate(((low, after), (high, before), (high, after), (low, before)))
        ]
        up, down = strips.at[before, u, low], strips.at[after, u, high]
        return near + [copy(up, up, after, 4), copy(down, down, before, 5)]

    def strip_begin(u):
        for entry in strip_copies(u)[:4]:
            entry().start()

    def strip_pass(u):
        sent = strip_copies(u)
        sent[0]().wait_recv()
        sent[4]().start()
        sent[1]().wait_recv()
        sent[5]().start()

    def strip_finish(u):
        sent = strip_copies(u)
        for i in range(2, 6):
            sent[i]().wait_recv()
        for entry in sent:
            entry().wait_send()

    keep = pltpu.make_async_copy(strip_ref, strips.at[col], keep_sem)

    def share_copy(n, e):
        to = base + e
        to_core, to_major, to_minor = place(to)
        return pltpu.make_async_remote_copy(
            src_ref=rounded_ref.at[pl.ds(e * share, share), lanes(n)],
            dst_ref=side_ref.at[to_core, to_major, to_minor, :, lanes(n)],
            send_sem=share_send.at[n, e],
            recv_sem=share_recv.at[n],
            device_id=(to, col),
            device_id_type=MESH,
        )

    def share_keep(n):
        return pltpu.make_async_copy(
            rounded_ref.at[pl.ds(pl.multiple_of(col * share, share), share), lanes(n)],
            side_ref.at[core, major, minor, :, lanes(n)],
            share_own,
        )

    def put_inverse(k, at_r, at_c, value):
        high, low = pieces(value)
        for start, part in ((0, high), (B, low), (2 * B, high)):
            inverse[k, at_r : at_r + H, start + at_c : start + at_c + H] = part

    def solve(n):
        acc[...] = strips[n % 4, n // 4]

        def update(j, carry):
            acc[...] -= dot_bf(rounded_ref[:, lanes(j)], lead[index_of(n, j)], NT)
            return carry

        lax.fori_loop(0, n, update, 0)
        solved = dot_inverse(acc[...], inverse[n])
        later = (at_row >= B) | (n < tile)
        rounded_ref[:, lanes(n)] = jnp.where(later, solved, 0.0).astype(BF16)

        @pl.when(n % 4 == col)
        def _():
            kept = later | ((n == tile) & (at_col <= at_row))
            panel_ref[n // 4] = jnp.where(kept, solved, 0.0)

        for e in range(4):
            when(is_source & (col != e), lambda e=e: share_copy(n, e).start())
        when(is_source, lambda: share_keep(n).start())

    def side_begin(n):
        when(is_source, lambda: share_keep(n).wait())
        when(jnp.logical_not(is_source), lambda: share_copy(n, (row + 1) % 4).wait_recv())
        side_walk.begin(n)

    def side_finish(n):
        side_walk.finish(n)
        for e in range(4):
            when(is_source & (col != e), lambda e=e: share_copy(n, e).wait_send())

    partners = [(row_of(core, major, (minor + d) % 4), col) for d in (1, 2, 3)]
    partners += [(row_of(core, (major + d) % 4, minor), col) for d in (1, 3)]
    partners += [(row + 1 - 2 * core, col)]
    partners += [(base + (row + d) % 4, col) for d in (1, 2, 3)]
    partners += [(row, (col + d) % 4) for d in (1, 2, 3)]
    barrier = pltpu.get_barrier_semaphore()
    for device in partners:
        pl.semaphore_signal(barrier, inc=1, device_id=device, device_id_type=MESH)
    for to in range(STEPS):
        @pl.when((col <= to) & (row != to))
        def _(to=to):
            pl.semaphore_signal(barrier, inc=1, device_id=(to, col), device_id_type=MESH)
    owner = (row < STEPS) & (col <= row)
    pl.semaphore_wait(barrier, len(partners) + 31 * owner.astype(jnp.int32))

    each_fill(lambda entry: entry.start())
    for u in range(2):
        when(mine[u][2], lambda u=u: fill_own(u).start())
    onward_begin(0)
    strip_begin(0)
    keep.start()
    lead_begin(0)
    onward_begin(1)
    lead_walk.second(0)
    lead_walk.third(0)
    lead_walk.fourth(0)
    lead_walk.finish(0)
    onward_finish(0)
    keep.wait()

    def step(k, carry):
        when(k == 4, lambda: lead_walk.finish(1))
        when(k == 4, lambda: onward_finish(1))
        at = tile_at(k, k)

        def row_tile(j, carry):
            here = tile_at(k, j)

            def update(i, carry):
                tiles[here] -= dot_bf(lead[index_of(k, i)], lead[index_of(j, i)], NT)
                return carry

            lax.fori_loop(0, j, update, 0)
            found = dot_inverse(tiles[here], inverse[j]).astype(BF16)
            lead[index_of(k, j)] = found
            tiles[at] -= dot_bf(found, found, NT)
            return carry

        lax.fori_loop(0, k, row_tile, 0)

        @pl.when(k == 1)
        def _():
            strip_finish(0)

        @pl.when(k == 5)
        def _():
            strip_finish(1)

        when(k >= 1, lambda: solve(k - 1))

        def half_step(h, carry):
            def at_half(value, condition, action):
                pl.when((h == value) & condition)(action)

            def early():
                at_half(0, k == 0, lambda: lead_begin(1))

            def middle():
                at_half(0, k >= 3, lambda: side_finish(k - 3))
                at_half(0, k >= 2, lambda: side_walk.third(k - 2))
                at_half(0, k >= 1, lambda: side_begin(k - 1))
                at_half(0, k == 0, lambda: strip_pass(0))
                at_half(1, k >= 2, lambda: side_walk.fourth(k - 2))
                at_half(1, k >= 1, lambda: side_walk.second(k - 1))

            def late():
                at_half(0, k == 0, lambda: lead_walk.second(1))

            @pl.when(h == 0)
            def _():
                diag[...] = tiles[at, 0:H, 0:H]

            done = inverse_factor([diag[8 * g : 8 * g + 8, :] for g in range(16)], {4: early, 10: middle, 14: late})
            for g in range(16):
                inv_half[8 * g : 8 * g + 8, :] = done[g]

            @pl.when(h == 0)
            def _():
                when(k == 1, lambda: lead_walk.third(1))
                when(k == 1, lambda: strip_begin(1))
                when(k == 2, lambda: lead_walk.fourth(1))
                when(k == 3, lambda: strip_pass(1))
                first = inv_half[...]
                l21 = dot_full(tiles[at, H:B, 0:H], first, NT)
                diag[...] = tiles[at, H:B, H:B] - dot_full(l21, l21, NT)
                mixed[...] = dot_full(l21, first, NN)
                put_inverse(k, 0, 0, first)
                put_inverse(k, 0, H, jnp.zeros((H, H), F32))

            @pl.when(h == 1)
            def _():
                second = inv_half[...]
                put_inverse(k, H, 0, -dot_full(second, mixed[...], NN))
                put_inverse(k, H, H, second)

            return carry

        return lax.fori_loop(0, 2, half_step, carry)

    lax.fori_loop(0, STEPS, step, 0)
    last = STEPS - 1
    solve(last)
    side_finish(last - 2)
    side_walk.third(last - 1)
    side_begin(last)
    side_walk.fourth(last - 1)
    side_walk.second(last)
    side_finish(last - 1)
    side_walk.third(last)
    side_walk.fourth(last)
    side_finish(last)
    each_fill(lambda entry: entry.wait_send())


def factor(strip):
    vmem = pl.BlockSpec(memory_space=pltpu.VMEM)
    anywhere = pl.BlockSpec(memory_space=pl.ANY)
    dma = pltpu.SemaphoreType.DMA
    return pl.pallas_call(
        factor_kernel,
        out_shape=(
            jax.ShapeDtypeStruct((2, 2 * B, B), F32),
            jax.ShapeDtypeStruct((2 * B, STEPS * B), BF16),
            jax.ShapeDtypeStruct((2, 4, 4, H, STEPS * B), BF16),
        ),
        in_specs=[anywhere],
        out_specs=(vmem, vmem, anywhere),
        scratch_shapes=[
            pltpu.VMEM((28, B, B), F32),
            pltpu.VMEM((4, 2, 2 * B, B), F32),
            pltpu.VMEM((28, B, B), BF16),
            pltpu.VMEM((STEPS, B, 3 * B), BF16),
            pltpu.VMEM((H, H), F32),
            pltpu.VMEM((H, H), F32),
            pltpu.VMEM((H, H), F32),
            pltpu.VMEM((2 * B, B), F32),
            dma((2, 32)), dma((2,)), dma((2, 4)), dma((2, 4)), dma, dma((STEPS, 4)), dma((STEPS,)), dma,
            dma((2, 6)), dma((2, 6)), dma((2, 13)), dma((2, 13)), dma((STEPS, 13)), dma((STEPS, 13)),
        ],
        compiler_params=pltpu.CompilerParams(
            has_side_effects=True, collective_id=0, vmem_limit_bytes=48 * 2**20
        ),
    )(strip)


def trailing_kernel(matrix_ref, nugget_ref, panel_ref, rounded_ref, even_ref, odd_ref, out_ref):
    slot = pl.program_id(0)
    tile, col = lax.axis_index("row"), lax.axis_index("col")
    col_tile = slot * 4 + col

    @pl.when(col_tile < STEPS)
    def _():
        out_ref[...] = panel_ref[0]

    @pl.when(col_tile >= STEPS)
    def _():
        side = jnp.concatenate([even_ref[0, 0, 0], odd_ref[0, 0, 0]], axis=0)
        out_ref[...] = matrix_ref[...] - dot_bf(rounded_ref[...], side, NT)
        for s in range(2):
            rows = pl.ds(s * B, B)

            @pl.when(col_tile == s * 32 + tile)
            def _(s=s, rows=rows):
                at_row = lax.broadcasted_iota(jnp.int32, (B, B), 0)
                at_col = lax.broadcasted_iota(jnp.int32, (B, B), 1)
                out_ref[rows, :] += jnp.where(at_row == at_col, nugget_ref[s : s + 1, :], 0.0)

        @pl.when(tile < STEPS)
        def _():
            out_ref[0:B, :] = jnp.zeros((B, B), F32)


def trailing(matrix, nugget, panel, rounded, side):
    rows, cols = matrix.shape
    depth = rounded.shape[1]

    def even(t):
        return (0, t % 8 // 2, 2 * (t % 2) + t // 8, 0, 0)

    def odd(t):
        return (1, 2 * (t % 2) + t // 8, t % 8 // 2, 0, 0)

    return pl.pallas_call(
        trailing_kernel,
        grid=(cols // B,),
        out_shape=jax.ShapeDtypeStruct(matrix.shape, F32),
        in_specs=[
            pl.BlockSpec((rows, B), lambda t: (0, t)),
            pl.BlockSpec((2, B), lambda t: (0, 0)),
            pl.BlockSpec((1, rows, B), lambda t: (jnp.minimum(t, 1), 0, 0)),
            pl.BlockSpec((rows, depth), lambda t: (0, 0)),
            pl.BlockSpec((1, 1, 1, H, depth), even),
            pl.BlockSpec((1, 1, 1, H, depth), odd),
        ],
        out_specs=pl.BlockSpec((rows, B), lambda t: (0, t)),
        compiler_params=pltpu.CompilerParams(vmem_limit_bytes=48 * 2**20),
    )(matrix, nugget, panel, rounded, side, side)


def body(kernel, nugget):
    rows_here = kernel.shape[0]
    tile, col = lax.axis_index("row"), lax.axis_index("col")
    nugget = nugget.reshape(2, B)
    strip = kernel[:, : 2 * B].reshape(rows_here, 2, B).transpose(1, 0, 2)
    col_tile = jnp.arange(2)[:, None, None] * 4 + col
    same = (
        (col_tile == tile)
        & (jnp.arange(rows_here)[None, :, None] == jnp.arange(B)[None, None, :])
    )
    strip = strip + jnp.where(same, nugget[0][None, None, :], 0.0)
    panel, rounded, side = factor(strip)
    return trailing(kernel, nugget, panel, rounded, side)


def solution(mesh):
    return jax.shard_map(
        body,
        mesh=mesh,
        in_specs=(P("row", "col"), P("row")),
        out_specs=P("row", "col"),
        check_vma=False,
    )
```

```python
import jax
import jax.numpy as jnp
from jax import lax
from jax.experimental import pallas as pl
from jax.experimental.pallas import tpu as pltpu
from jax.sharding import PartitionSpec as P

B = 256
H = 128
STEPS = 7
WIDE = 4
F32 = jnp.float32
BF16 = jnp.bfloat16
MESH = pl.DeviceIdType.MESH
NT = (((1,), (1,)), ((), ()))
NN = (((1,), (0,)), ((), ()))


def pieces(x):
    high = x.astype(BF16)
    return high, (x - high.astype(F32)).astype(BF16)


def dot_full(a, b, dims):
    a_high, a_low = pieces(a)
    b_high, b_low = pieces(b)
    a_axis, b_axis = dims[0][0][0], dims[0][1][0]
    return dot_bf(
        jnp.concatenate([a_high, a_high, a_low], axis=a_axis),
        jnp.concatenate([b_high, b_low, b_high], axis=b_axis),
        dims,
    )


def dot_inverse(a, terms):
    high, low = pieces(a)
    return dot_bf(jnp.concatenate([high, high, low], axis=1), terms, NT)


def dot_bf(a, b, dims):
    return lax.dot_general(a, b, dims, preferred_element_type=F32)


def lane_splat(x, at):
    return jnp.broadcast_to(x[:, at : at + 1], x.shape)


def row_splat(x, at):
    return jnp.broadcast_to(x[at : at + 1, :], x.shape)


def inverse_factor(groups, hooks):
    lane = lax.broadcasted_iota(jnp.int32, (8, H), 1)
    sub = lax.broadcasted_iota(jnp.int32, (8, H), 0)
    groups = list(groups)
    result = []
    for b in range(16):
        if b in hooks:
            hooks[b]()
        start = 8 * b
        block = (lane >= start) & (lane < start + 8)
        here = groups[b]
        cols = [lane_splat(here, start + s) for s in range(8)]
        swept = jnp.where(block, jnp.where(lane - start == sub, 1.0, 0.0), here)
        scaled = pivots = jnp.ones((8, H), F32)
        for r in range(0, 8, 2):
            a, c, d = row_splat(cols[r], r), row_splat(cols[r + 1], r), row_splat(cols[r + 1], r + 1)
            det = a * d - c * c
            inv = 1.0 / det
            at_0, at_1 = sub == r, sub == r + 1
            inv_a = 1.0 / a

            def sweep(x):
                u, v = row_splat(x, r), row_splat(x, r + 1)
                first, second = (d * u - c * v) * inv, (a * v - c * u) * inv
                rest = x - (cols[r] * first + cols[r + 1] * second)
                return jnp.where(at_0, first, jnp.where(at_1, second, rest)), u, v

            new, u, v = sweep(swept)
            scaled = jnp.where(at_0, u, jnp.where(at_1, v - (c * inv_a) * u, scaled))
            pivots = jnp.where(at_0, a, jnp.where(at_1, det * inv_a, pivots))
            swept = new
            for j in range(r + 2, 8):
                cols[j] = sweep(cols[j])[0]
        result.append(jnp.where(lane <= sub + start, scaled * lax.rsqrt(pivots), 0.0))
        rows = [row_splat(swept, s) for s in range(8)]
        near = min(b + 1, 15)
        if near < 15:
            zero = jnp.zeros((8, H), F32)
            spread = jnp.concatenate([swept if g == b else zero for g in range(16)], axis=0)
            far = dot_full(jnp.concatenate(groups[near + 1 :], axis=0), spread, NN)
        for g in range(b + 1, near + 1):
            terms = [lane_splat(groups[g], start + s) * rows[s] for s in range(8)]
            while len(terms) > 1:
                terms = [terms[i] + terms[i + 1] for i in range(0, len(terms), 2)]
            groups[g] = jnp.where(block, 0.0, groups[g]) - terms[0]
        for g in range(near + 1, 16):
            at = 8 * (g - near - 1)
            groups[g] = jnp.where(block, 0.0, groups[g]) - far[at : at + 8]
    return result


def place(row):
    core, y, x = row % 2, row // 2 % 4, row // 8
    return core, x * (1 - core) + y * core, y * (1 - core) + x * core


def row_of(core, major, minor):
    x = major * (1 - core) + minor * core
    y = minor * (1 - core) + major * core
    return (x * 4 + y) * 2 + core


class Walk:
    def __init__(self, single, low, high, whole, send, recv, direct=False):
        self.row, self.col = lax.axis_index("row"), lax.axis_index("col")
        self.core, self.major, self.minor = place(self.row)
        self.parts = single, low, high, whole
        self.send, self.recv, self.direct = send, recv, direct

    def copies(self, n):
        single, low, high, whole = self.parts
        core, major, minor = self.core, self.major, self.minor

        def copy(ref, device, slot):
            return lambda: pltpu.make_async_remote_copy(
                src_ref=ref,
                dst_ref=ref,
                send_sem=self.send.at[n, slot],
                recv_sem=self.recv.at[n, slot],
                device_id=(device, self.col),
                device_id_type=MESH,
            )

        first = [
            copy(single(n, minor), row_of(core, major, (minor + d) % 4), i) for i, d in enumerate((1, 3, 2))
        ]
        after, before = (major + 1) % 4, (major + 3) % 4
        up, down = row_of(core, after, minor), row_of(core, before, minor)
        second = [
            copy(low(n, major), up, 3),
            copy(high(n, major), down, 4),
            copy(high(n, major), up, 5),
            copy(low(n, major), down, 6),
            copy(low(n, before), up, 7),
            copy(high(n, after), down, 8),
        ]
        if self.direct:
            block = whole(n, major)
            second = [copy(block, row_of(core, (major + d) % 4, minor), 3 + i) for i, d in enumerate((1, 3, 2))]
        sibling = self.row + 1 - 2 * core
        order = (major, before, after, (major + 2) % 4)
        start = 3 + len(second)
        return first + second + [copy(whole(n, at), sibling, start + i) for i, at in enumerate(order)]

    def begin(self, n):
        sent = self.copies(n)
        for i in (2, 0, 1):
            sent[i]().start()

    def second(self, n):
        sent = self.copies(n)
        for i in range(3):
            sent[i]().wait_recv()
        for i in (5, 3, 4, 6) if self.direct else (3, 4, 5, 6, 9):
            sent[i]().start()

    def third(self, n):
        sent = self.copies(n)
        if self.direct:
            for i in range(3, 6):
                sent[i]().wait_recv()
                sent[i + 4]().start()
            return
        sent[3]().wait_recv()
        sent[7]().start()
        sent[4]().wait_recv()
        sent[8]().start()
        sent[5]().wait_recv()
        sent[10]().start()
        sent[6]().wait_recv()
        sent[11]().start()

    def fourth(self, n):
        sent = self.copies(n)
        sent[7]().wait_recv()
        sent[8]().wait_recv()
        sent[12]().start()

    def finish(self, n):
        sent = self.copies(n)
        for entry in sent[-4:]:
            entry().wait_recv()
        for entry in sent:
            entry().wait_send()


GROUP_START = (0, 10)
GROUP_SIZE = (10, 18)
FROM_PLANE = ((4, 3, 2, 1), (6, 5, 4, 3))


def from_plane_start(group, plane):
    return GROUP_START[group] + sum(FROM_PLANE[group][:plane])


def tile_at(i, j):
    plane = j % 4
    early = 4 * j - j * (j - 1) // 2 + i - j
    late = 10 + 6 * plane - plane * (plane - 1) // 2 + jnp.where(j < 4, i - 4, 3 + i - j)
    return jnp.where(i < 4, early, late)


def index_of(i, j):
    return i * (i + 1) // 2 + j


def lanes(k):
    return pl.ds(pl.multiple_of(k * B, B), B)


def factor_kernel(
    matrix_ref, nugget_ref, panel_ref, rounded_ref, side_ref,
    tiles, strips, lead, inverse, diag, inv_half, mixed, acc,
    fill_send, fill_recv, onward_send, onward_recv, keep_sem, share_send, share_recv, share_own,
    strip_send, strip_recv, lead_send, lead_recv, side_send, side_recv,
):
    row, col = lax.axis_index("row"), lax.axis_index("col")
    core, major, minor = place(row)
    tile = row
    base = row // 4 * 4
    is_source = row % 4 == col
    share = rounded_ref.shape[0] // 4
    at_row = lax.broadcasted_iota(jnp.int32, (2 * B, B), 0)
    at_col = lax.broadcasted_iota(jnp.int32, (2 * B, B), 1)

    def when(condition, action):
        @pl.when(condition)
        def _():
            action()

    def span(start, size):
        return pl.ds(pl.multiple_of(start, 8), size)

    def group_tiles(g):
        return pl.ds(GROUP_START[g], GROUP_SIZE[g])

    lead_walk = Walk(
        lambda g, at: tiles.at[group_tiles(g), span(8 * (core * 16 + major * 4 + at), 8)],
        lambda g, at: tiles.at[group_tiles(g), span(8 * (core * 16 + at * 4), 16)],
        lambda g, at: tiles.at[group_tiles(g), span(8 * (core * 16 + at * 4) + 16, 16)],
        lambda g, at: tiles.at[group_tiles(g), span(8 * (core * 16 + at * 4), 32)],
        lead_send,
        lead_recv,
    )
    half = 2
    side_walk = Walk(
        lambda n, at: side_ref.at[core, major, at, :, lanes(n)],
        lambda n, at: side_ref.at[core, at, pl.ds(0, half), :, lanes(n)],
        lambda n, at: side_ref.at[core, at, pl.ds(half, half), :, lanes(n)],
        lambda n, at: side_ref.at[core, at, :, :, lanes(n)],
        side_send,
        side_recv,
    )

    piece = span(8 * (core * 16 + major * 4 + minor), 8)
    mine = []
    for u in range(2):
        mine.append((tile_at(row, col + 4 * u), (row >= 4).astype(jnp.int32), (row < STEPS) & (col + 4 * u <= row)))

    def fill(u, to):
        to_core, to_major, to_minor = place(to)
        there = span(8 * (to_core * 16 + to_major * 4 + to_minor), 8)
        return pltpu.make_async_remote_copy(
            src_ref=strips.at[col, u, there],
            dst_ref=tiles.at[mine[u][0], there],
            send_sem=fill_send.at[u, to],
            recv_sem=fill_recv.at[mine[u][1]],
            device_id=(to, col),
            device_id_type=MESH,
        )

    def fill_own(u):
        return pltpu.make_async_copy(
            strips.at[col, u, piece], tiles.at[mine[u][0], piece], fill_recv.at[mine[u][1]]
        )

    def each_fill(action):
        def one(to, carry):
            for u in range(2):
                when((to != row) & mine[u][2], lambda u=u: action(fill(u, to)))
            return carry

        when(row < STEPS, lambda: lax.fori_loop(0, 32, one, 0))

    def onward(g, plane, to):
        block = tiles.at[pl.ds(from_plane_start(g, plane), FROM_PLANE[g][plane]), piece]
        return pltpu.make_async_remote_copy(
            src_ref=block,
            dst_ref=block,
            send_sem=onward_send.at[g, to],
            recv_sem=onward_recv.at[g, plane],
            device_id=(row, to),
            device_id_type=MESH,
        )

    def onward_begin(g):
        for plane in range(4):
            @pl.when(col == plane)
            def _(plane=plane):
                block = tiles.at[pl.ds(from_plane_start(g, plane), FROM_PLANE[g][plane]), piece]
                pltpu.make_async_remote_copy(
                    src_ref=block,
                    dst_ref=block,
                    send_sem=onward_send.at[g, plane],
                    recv_sem=fill_recv.at[g],
                    device_id=(base + (row + 1) % 4, col),
                    device_id_type=MESH,
                ).wait_recv()
                for to in range(4):
                    if to != plane:
                        onward(g, plane, to).start()

    def lead_begin(g):
        for plane in range(4):
            when(col != plane, lambda plane=plane: onward(g, plane, (plane + 1) % 4).wait_recv())
        lead_walk.begin(g)

    def onward_finish(g):
        for plane in range(4):
            @pl.when(col == plane)
            def _(plane=plane):
                for to in range(4):
                    if to != plane:
                        onward(g, plane, to).wait_send()

    def strip_copies(u):
        after, before = (col + 1) % 4, (col + 3) % 4

        def copy(src, dst, to, slot):
            return lambda: pltpu.make_async_remote_copy(
                src_ref=src,
                dst_ref=dst,
                send_sem=strip_send.at[u, slot],
                recv_sem=strip_recv.at[u, slot],
                device_id=(row, to),
                device_id_type=MESH,
            )

        low, high = pl.ds(0, B), pl.ds(B, B)
        near = [
            copy(strips.at[col, u, part], strips.at[col, u, part], to, slot)
            for slot, (part, to) in enumerate(((low, after), (high, before), (high, after), (low, before)))
        ]
        up, down = strips.at[before, u, low], strips.at[after, u, high]
        return near + [copy(up, up, after, 4), copy(down, down, before, 5)]

    def strip_begin(u):
        for entry in strip_copies(u)[:4]:
            entry().start()

    def strip_pass(u):
        sent = strip_copies(u)
        sent[0]().wait_recv()
        sent[4]().start()
        sent[1]().wait_recv()
        sent[5]().start()

    def strip_finish(u):
        sent = strip_copies(u)
        for i in range(2, 6):
            sent[i]().wait_recv()
        for entry in sent:
            entry().wait_send()

    def keep(u):
        return pltpu.make_async_copy(matrix_ref.at[:, pl.ds(u * B, B)], strips.at[col, u], keep_sem.at[u])

    def share_copy(n, e):
        to = base + e
        to_core, to_major, to_minor = place(to)
        return pltpu.make_async_remote_copy(
            src_ref=rounded_ref.at[pl.ds(e * share, share), lanes(n)],
            dst_ref=side_ref.at[to_core, to_major, to_minor, :, lanes(n)],
            send_sem=share_send.at[n, e],
            recv_sem=share_recv.at[n],
            device_id=(to, col),
            device_id_type=MESH,
        )

    def share_keep(n):
        return pltpu.make_async_copy(
            rounded_ref.at[pl.ds(pl.multiple_of(col * share, share), share), lanes(n)],
            side_ref.at[core, major, minor, :, lanes(n)],
            share_own,
        )

    def put_inverse(k, at_r, at_c, value):
        high, low = pieces(value)
        for start, part in ((0, high), (B, low), (2 * B, high)):
            inverse[k, at_r : at_r + H, start + at_c : start + at_c + H] = part

    def solve(n):
        acc[...] = strips[n % 4, n // 4]

        def update(j, carry):
            acc[...] -= dot_bf(rounded_ref[:, lanes(j)], lead[index_of(n, j)], NT)
            return carry

        lax.fori_loop(0, n, update, 0)
        solved = dot_inverse(acc[...], inverse[n])
        later = (at_row >= B) | (n < tile)
        rounded_ref[:, lanes(n)] = jnp.where(later, solved, 0.0).astype(BF16)

        @pl.when(n % 4 == col)
        def _():
            kept = later | ((n == tile) & (at_col <= at_row))
            panel_ref[n // 4] = jnp.where(kept, solved, 0.0)

        for e in range(4):
            when(is_source & (col != e), lambda e=e: share_copy(n, e).start())
        when(is_source, lambda: share_keep(n).start())

    def side_begin(n):
        when(is_source, lambda: share_keep(n).wait())
        when(jnp.logical_not(is_source), lambda: share_copy(n, (row + 1) % 4).wait_recv())
        side_walk.begin(n)

    def side_finish(n):
        side_walk.finish(n)
        for e in range(4):
            when(is_source & (col != e), lambda e=e: share_copy(n, e).wait_send())

    for u in range(2):
        keep(u).start()

    partners = [(row_of(core, major, (minor + d) % 4), col) for d in (1, 2, 3)]
    partners += [(row_of(core, (major + d) % 4, minor), col) for d in (1, 2, 3)]
    partners += [(row + 1 - 2 * core, col)]
    partners += [(base + (row + d) % 4, col) for d in (1, 2, 3)]
    partners += [(row, (col + d) % 4) for d in (1, 2, 3)]
    barrier = pltpu.get_barrier_semaphore()
    for device in partners:
        pl.semaphore_signal(barrier, inc=1, device_id=device, device_id_type=MESH)
    for to in range(STEPS):
        @pl.when((col <= to) & (row != to))
        def _(to=to):
            pl.semaphore_signal(barrier, inc=1, device_id=(to, col), device_id_type=MESH)
    for u in range(2):
        keep(u).wait()

        @pl.when(col + 4 * u == row)
        def _(u=u):
            strips[col, u, 0:B] += jnp.where(at_row[0:B] == at_col[0:B], nugget_ref[:, 0:B], 0.0)

    owner = (row < STEPS) & (col <= row)
    pl.semaphore_wait(barrier, len(partners) + 31 * owner.astype(jnp.int32))

    each_fill(lambda entry: entry.start())
    for u in range(2):
        when(mine[u][2], lambda u=u: fill_own(u).start())
    onward_begin(0)
    strip_begin(0)
    lead_begin(0)
    onward_begin(1)
    lead_walk.second(0)
    lead_walk.third(0)
    lead_walk.fourth(0)
    lead_walk.finish(0)
    onward_finish(0)

    def step(k, carry):
        when(k == 4, lambda: lead_walk.finish(1))
        when(k == 4, lambda: onward_finish(1))
        at = tile_at(k, k)

        def row_tile(j, carry):
            here = tile_at(k, j)

            def update(i, carry):
                tiles[here] -= dot_bf(lead[index_of(k, i)], lead[index_of(j, i)], NT)
                return carry

            lax.fori_loop(0, j, update, 0)
            found = dot_inverse(tiles[here], inverse[j]).astype(BF16)
            lead[index_of(k, j)] = found
            tiles[at] -= dot_bf(found, found, NT)
            return carry

        lax.fori_loop(0, k, row_tile, 0)

        @pl.when(k == 1)
        def _():
            strip_finish(0)

        @pl.when(k == 5)
        def _():
            strip_finish(1)

        when(k >= 1, lambda: solve(k - 1))

        def half_step(h, carry):
            def at_half(value, condition, action):
                pl.when((h == value) & condition)(action)

            def early():
                at_half(0, k >= 3, lambda: side_walk.fourth(k - 3))
                at_half(0, k == 0, lambda: lead_begin(1))
                at_half(1, k >= 3, lambda: side_finish(k - 3))
                at_half(1, k >= 2, lambda: side_walk.third(k - 2))
                at_half(1, k == 0, lambda: lead_walk.second(1))

            def late():
                at_half(0, k >= 1, lambda: side_begin(k - 1))
                at_half(0, k == 0, lambda: strip_pass(0))
                at_half(1, k >= 1, lambda: side_walk.second(k - 1))

            @pl.when(h == 0)
            def _():
                diag[...] = tiles[at, 0:H, 0:H]

            done = inverse_factor([diag[8 * g : 8 * g + 8, :] for g in range(16)], {3: early, 11: late})
            for g in range(16):
                inv_half[8 * g : 8 * g + 8, :] = done[g]

            @pl.when(h == 0)
            def _():
                when(k == 1, lambda: lead_walk.third(1))
                when(k == 2, lambda: lead_walk.fourth(1))
                when(k == 1, lambda: strip_begin(1))
                when(k == 3, lambda: strip_pass(1))
                first = inv_half[...]
                l21 = dot_full(tiles[at, H:B, 0:H], first, NT)
                diag[...] = tiles[at, H:B, H:B] - dot_full(l21, l21, NT)
                mixed[...] = dot_full(l21, first, NN)
                put_inverse(k, 0, 0, first)
                put_inverse(k, 0, H, jnp.zeros((H, H), F32))

            @pl.when(h == 1)
            def _():
                second = inv_half[...]
                put_inverse(k, H, 0, -dot_full(second, mixed[...], NN))
                put_inverse(k, H, H, second)

            return carry

        return lax.fori_loop(0, 2, half_step, carry)

    lax.fori_loop(0, STEPS, step, 0)
    last = STEPS - 1
    solve(last)
    side_walk.fourth(last - 2)
    side_walk.third(last - 1)
    side_begin(last)
    side_finish(last - 2)
    side_walk.fourth(last - 1)
    side_walk.second(last)
    side_finish(last - 1)
    side_walk.third(last)
    side_walk.fourth(last)
    side_finish(last)
    each_fill(lambda entry: entry.wait_send())


def factor(matrix, nugget):
    vmem = pl.BlockSpec(memory_space=pltpu.VMEM)
    anywhere = pl.BlockSpec(memory_space=pl.ANY)
    dma = pltpu.SemaphoreType.DMA
    return pl.pallas_call(
        factor_kernel,
        out_shape=(
            jax.ShapeDtypeStruct((2, 2 * B, B), F32),
            jax.ShapeDtypeStruct((2 * B, STEPS * B), BF16),
            jax.ShapeDtypeStruct((2, 4, 4, H, STEPS * B), BF16),
        ),
        in_specs=[anywhere, vmem],
        out_specs=(vmem, vmem, anywhere),
        scratch_shapes=[
            pltpu.VMEM((28, B, B), F32),
            pltpu.VMEM((4, 2, 2 * B, B), F32),
            pltpu.VMEM((28, B, B), BF16),
            pltpu.VMEM((STEPS, B, 3 * B), BF16),
            pltpu.VMEM((H, H), F32),
            pltpu.VMEM((H, H), F32),
            pltpu.VMEM((H, H), F32),
            pltpu.VMEM((2 * B, B), F32),
            dma((2, 32)), dma((2,)), dma((2, 4)), dma((2, 4)), dma((2,)), dma((STEPS, 4)), dma((STEPS,)), dma,
            dma((2, 6)), dma((2, 6)), dma((2, 13)), dma((2, 13)), dma((STEPS, 13)), dma((STEPS, 13)),
        ],
        compiler_params=pltpu.CompilerParams(
            has_side_effects=True, collective_id=0, vmem_limit_bytes=48 * 2**20
        ),
    )(matrix, nugget)


def trailing_kernel(matrix_ref, nugget_ref, panel_ref, rounded_ref, *refs):
    out_ref = refs[-1]
    tile, col = lax.axis_index("row"), lax.axis_index("col")
    for u in range(WIDE):
        even_ref, odd_ref = refs[2 * u], refs[2 * u + 1]
        slot = pl.program_id(0) * WIDE + u
        col_tile = slot * 4 + col
        here = slice(u * B, (u + 1) * B)

        @pl.when(col_tile < STEPS)
        def _(slot=slot, here=here):
            out_ref[:, here] = panel_ref[jnp.minimum(slot, 1)]

        @pl.when(col_tile >= STEPS)
        def _(even_ref=even_ref, odd_ref=odd_ref, col_tile=col_tile, here=here):
            side = jnp.concatenate([even_ref[0, 0, 0], odd_ref[0, 0, 0]], axis=0)
            out_ref[:, here] = matrix_ref[:, here] - dot_bf(rounded_ref[...], side, NT)
            for s in range(2):
                @pl.when(col_tile == s * 32 + tile)
                def _(s=s):
                    rows = slice(s * B, (s + 1) * B)
                    at_row = lax.broadcasted_iota(jnp.int32, (B, B), 0)
                    at_col = lax.broadcasted_iota(jnp.int32, (B, B), 1)
                    out_ref[rows, here] += jnp.where(at_row == at_col, nugget_ref[:, rows], 0.0)

            @pl.when(tile < STEPS)
            def _():
                out_ref[0:B, here] = jnp.zeros((B, B), F32)


def trailing(matrix, nugget, panel, rounded, side):
    rows, cols = matrix.shape
    depth = rounded.shape[1]

    def even(u):
        def at(g):
            t = g * WIDE + u
            return (0, t % 8 // 2, 2 * (t % 2) + t // 8, 0, 0)

        return at

    def odd(u):
        def at(g):
            t = g * WIDE + u
            return (1, 2 * (t % 2) + t // 8, t % 8 // 2, 0, 0)

        return at

    blocks = []
    for u in range(WIDE):
        blocks += [pl.BlockSpec((1, 1, 1, H, depth), even(u)), pl.BlockSpec((1, 1, 1, H, depth), odd(u))]
    return pl.pallas_call(
        trailing_kernel,
        grid=(cols // (WIDE * B),),
        out_shape=jax.ShapeDtypeStruct(matrix.shape, F32),
        in_specs=[
            pl.BlockSpec((rows, WIDE * B), lambda t: (0, t)),
            pl.BlockSpec((1, rows), lambda t: (0, 0)),
            pl.BlockSpec((2, rows, B), lambda t: (0, 0, 0)),
            pl.BlockSpec((rows, depth), lambda t: (0, 0)),
        ] + blocks,
        out_specs=pl.BlockSpec((rows, WIDE * B), lambda t: (0, t)),
        compiler_params=pltpu.CompilerParams(vmem_limit_bytes=48 * 2**20),
    )(matrix, nugget, panel, rounded, *([side] * (2 * WIDE)))


def body(kernel, nugget):
    nugget = nugget.reshape(1, kernel.shape[0])
    panel, rounded, side = factor(kernel, nugget)
    return trailing(kernel, nugget, panel, rounded, side)


def solution(mesh):
    return jax.shard_map(
        body,
        mesh=mesh,
        in_specs=(P("row", "col"), P("row")),
        out_specs=P("row", "col"),
        check_vma=False,
    )
```

```python
import jax
import jax.numpy as jnp
from jax import lax
from jax.experimental import pallas as pl
from jax.experimental.pallas import tpu as pltpu
from jax.sharding import PartitionSpec as P

B = 256
H = 128
STEPS = 7
WIDE = 2
F32 = jnp.float32
BF16 = jnp.bfloat16
MESH = pl.DeviceIdType.MESH
NT = (((1,), (1,)), ((), ()))
NN = (((1,), (0,)), ((), ()))


def pieces(x):
    high = x.astype(BF16)
    return high, (x - high.astype(F32)).astype(BF16)


def dot_full(a, b, dims):
    a_high, a_low = pieces(a)
    b_high, b_low = pieces(b)
    a_axis, b_axis = dims[0][0][0], dims[0][1][0]
    return dot_bf(
        jnp.concatenate([a_high, a_high, a_low], axis=a_axis),
        jnp.concatenate([b_high, b_low, b_high], axis=b_axis),
        dims,
    )


def dot_inverse(a, terms):
    high, low = pieces(a)
    return dot_bf(jnp.concatenate([high, high, low], axis=1), terms, NT)


def dot_bf(a, b, dims):
    return lax.dot_general(a, b, dims, preferred_element_type=F32)


def lane_splat(x, at):
    return jnp.broadcast_to(x[:, at : at + 1], x.shape)


def row_splat(x, at):
    return jnp.broadcast_to(x[at : at + 1, :], x.shape)


def inverse_factor(groups, hooks):
    lane = lax.broadcasted_iota(jnp.int32, (8, H), 1)
    sub = lax.broadcasted_iota(jnp.int32, (8, H), 0)
    groups = list(groups)
    result = []
    for b in range(16):
        if b in hooks:
            hooks[b]()
        start = 8 * b
        block = (lane >= start) & (lane < start + 8)
        here = groups[b]
        cols = [lane_splat(here, start + s) for s in range(8)]
        swept = jnp.where(block, jnp.where(lane - start == sub, 1.0, 0.0), here)
        scaled = pivots = jnp.ones((8, H), F32)
        for r in range(0, 8, 2):
            a, c, d = row_splat(cols[r], r), row_splat(cols[r + 1], r), row_splat(cols[r + 1], r + 1)
            det = a * d - c * c
            inv = 1.0 / det
            at_0, at_1 = sub == r, sub == r + 1
            inv_a = 1.0 / a

            def sweep(x):
                u, v = row_splat(x, r), row_splat(x, r + 1)
                first, second = (d * u - c * v) * inv, (a * v - c * u) * inv
                rest = x - (cols[r] * first + cols[r + 1] * second)
                return jnp.where(at_0, first, jnp.where(at_1, second, rest)), u, v

            new, u, v = sweep(swept)
            scaled = jnp.where(at_0, u, jnp.where(at_1, v - (c * inv_a) * u, scaled))
            pivots = jnp.where(at_0, a, jnp.where(at_1, det * inv_a, pivots))
            swept = new
            for j in range(r + 2, 8):
                cols[j] = sweep(cols[j])[0]
        result.append(jnp.where(lane <= sub + start, scaled * lax.rsqrt(pivots), 0.0))
        rows = [row_splat(swept, s) for s in range(8)]
        near = min(b + 1, 15)
        if near < 15:
            zero = jnp.zeros((8, H), F32)
            spread = jnp.concatenate([swept if g == b else zero for g in range(16)], axis=0)
            far = dot_full(jnp.concatenate(groups[near + 1 :], axis=0), spread, NN)
        for g in range(b + 1, near + 1):
            terms = [lane_splat(groups[g], start + s) * rows[s] for s in range(8)]
            while len(terms) > 1:
                terms = [terms[i] + terms[i + 1] for i in range(0, len(terms), 2)]
            groups[g] = jnp.where(block, 0.0, groups[g]) - terms[0]
        for g in range(near + 1, 16):
            at = 8 * (g - near - 1)
            groups[g] = jnp.where(block, 0.0, groups[g]) - far[at : at + 8]
    return result


def place(row):
    core, y, x = row % 2, row // 2 % 4, row // 8
    return core, x * (1 - core) + y * core, y * (1 - core) + x * core


def row_of(core, major, minor):
    x = major * (1 - core) + minor * core
    y = minor * (1 - core) + major * core
    return (x * 4 + y) * 2 + core


class Walk:
    def __init__(self, single, low, high, whole, send, recv, direct=False):
        self.row, self.col = lax.axis_index("row"), lax.axis_index("col")
        self.core, self.major, self.minor = place(self.row)
        self.parts = single, low, high, whole
        self.send, self.recv, self.direct = send, recv, direct

    def copies(self, n):
        single, low, high, whole = self.parts
        core, major, minor = self.core, self.major, self.minor

        def copy(ref, device, slot):
            return lambda: pltpu.make_async_remote_copy(
                src_ref=ref,
                dst_ref=ref,
                send_sem=self.send.at[n, slot],
                recv_sem=self.recv.at[n, slot],
                device_id=(device, self.col),
                device_id_type=MESH,
            )

        first = [
            copy(single(n, minor), row_of(core, major, (minor + d) % 4), i) for i, d in enumerate((1, 3, 2))
        ]
        after, before = (major + 1) % 4, (major + 3) % 4
        up, down = row_of(core, after, minor), row_of(core, before, minor)
        second = [
            copy(low(n, major), up, 3),
            copy(high(n, major), down, 4),
            copy(high(n, major), up, 5),
            copy(low(n, major), down, 6),
            copy(low(n, before), up, 7),
            copy(high(n, after), down, 8),
        ]
        if self.direct:
            block = whole(n, major)
            second = [copy(block, row_of(core, (major + d) % 4, minor), 3 + i) for i, d in enumerate((1, 3, 2))]
        sibling = self.row + 1 - 2 * core
        order = (major, before, after, (major + 2) % 4)
        start = 3 + len(second)
        return first + second + [copy(whole(n, at), sibling, start + i) for i, at in enumerate(order)]

    def begin(self, n):
        sent = self.copies(n)
        for i in (2, 0, 1):
            sent[i]().start()

    def second(self, n):
        sent = self.copies(n)
        for i in range(3):
            sent[i]().wait_recv()
        for i in (5, 3, 4, 6) if self.direct else (3, 4, 5, 6, 9):
            sent[i]().start()

    def third(self, n):
        sent = self.copies(n)
        if self.direct:
            for i in range(3, 6):
                sent[i]().wait_recv()
                sent[i + 4]().start()
            return
        sent[3]().wait_recv()
        sent[7]().start()
        sent[4]().wait_recv()
        sent[8]().start()
        sent[5]().wait_recv()
        sent[10]().start()
        sent[6]().wait_recv()
        sent[11]().start()

    def fourth(self, n):
        sent = self.copies(n)
        sent[7]().wait_recv()
        sent[8]().wait_recv()
        sent[12]().start()

    def finish(self, n):
        sent = self.copies(n)
        for entry in sent[-4:]:
            entry().wait_recv()
        for entry in sent:
            entry().wait_send()


GROUP_START = (0, 10)
GROUP_SIZE = (10, 18)
FROM_PLANE = ((4, 3, 2, 1), (6, 5, 4, 3))


def from_plane_start(group, plane):
    return GROUP_START[group] + sum(FROM_PLANE[group][:plane])


def tile_at(i, j):
    plane = j % 4
    early = 4 * j - j * (j - 1) // 2 + i - j
    late = 10 + 6 * plane - plane * (plane - 1) // 2 + jnp.where(j < 4, i - 4, 3 + i - j)
    return jnp.where(i < 4, early, late)


def index_of(i, j):
    return i * (i + 1) // 2 + j


def lanes(k):
    return pl.ds(pl.multiple_of(k * B, B), B)


def factor_kernel(
    matrix_ref, nugget_hbm, panel_ref, rounded_ref, side_ref,
    nugget_ref, tiles, strips, lead, inverse, diag, inv_half, mixed, acc,
    fill_send, fill_recv, onward_send, onward_recv, keep_sem, share_send, share_recv, share_own,
    strip_send, strip_recv, lead_send, lead_recv, side_send, side_recv,
):
    row, col = lax.axis_index("row"), lax.axis_index("col")
    core, major, minor = place(row)
    tile = row
    base = row // 4 * 4
    is_source = row % 4 == col
    share = rounded_ref.shape[0] // 4
    at_row = lax.broadcasted_iota(jnp.int32, (2 * B, B), 0)
    at_col = lax.broadcasted_iota(jnp.int32, (2 * B, B), 1)

    def when(condition, action):
        @pl.when(condition)
        def _():
            action()

    def span(start, size):
        return pl.ds(pl.multiple_of(start, 8), size)

    def group_tiles(g):
        return pl.ds(GROUP_START[g], GROUP_SIZE[g])

    lead_walk = Walk(
        lambda g, at: tiles.at[group_tiles(g), span(8 * (core * 16 + major * 4 + at), 8)],
        lambda g, at: tiles.at[group_tiles(g), span(8 * (core * 16 + at * 4), 16)],
        lambda g, at: tiles.at[group_tiles(g), span(8 * (core * 16 + at * 4) + 16, 16)],
        lambda g, at: tiles.at[group_tiles(g), span(8 * (core * 16 + at * 4), 32)],
        lead_send,
        lead_recv,
    )
    half = 2
    side_walk = Walk(
        lambda n, at: side_ref.at[core, major, at, :, lanes(n)],
        lambda n, at: side_ref.at[core, at, pl.ds(0, half), :, lanes(n)],
        lambda n, at: side_ref.at[core, at, pl.ds(half, half), :, lanes(n)],
        lambda n, at: side_ref.at[core, at, :, :, lanes(n)],
        side_send,
        side_recv,
    )

    piece = span(8 * (core * 16 + major * 4 + minor), 8)
    mine = []
    for u in range(2):
        mine.append((tile_at(row, col + 4 * u), (row >= 4).astype(jnp.int32), (row < STEPS) & (col + 4 * u <= row)))

    def fill(u, to):
        to_core, to_major, to_minor = place(to)
        there = span(8 * (to_core * 16 + to_major * 4 + to_minor), 8)
        return pltpu.make_async_remote_copy(
            src_ref=strips.at[col, u, there],
            dst_ref=tiles.at[mine[u][0], there],
            send_sem=fill_send.at[u, to],
            recv_sem=fill_recv.at[mine[u][1]],
            device_id=(to, col),
            device_id_type=MESH,
        )

    def fill_own(u):
        return pltpu.make_async_copy(
            strips.at[col, u, piece], tiles.at[mine[u][0], piece], fill_recv.at[mine[u][1]]
        )

    def each_fill(action):
        def one(to, carry):
            for u in range(2):
                when((to != row) & mine[u][2], lambda u=u: action(fill(u, to)))
            return carry

        when(row < STEPS, lambda: lax.fori_loop(0, 32, one, 0))

    def onward(g, plane, to):
        block = tiles.at[pl.ds(from_plane_start(g, plane), FROM_PLANE[g][plane]), piece]
        return pltpu.make_async_remote_copy(
            src_ref=block,
            dst_ref=block,
            send_sem=onward_send.at[g, to],
            recv_sem=onward_recv.at[g, plane],
            device_id=(row, to),
            device_id_type=MESH,
        )

    def onward_begin(g):
        for plane in range(4):
            @pl.when(col == plane)
            def _(plane=plane):
                block = tiles.at[pl.ds(from_plane_start(g, plane), FROM_PLANE[g][plane]), piece]
                pltpu.make_async_remote_copy(
                    src_ref=block,
                    dst_ref=block,
                    send_sem=onward_send.at[g, plane],
                    recv_sem=fill_recv.at[g],
                    device_id=(base + (row + 1) % 4, col),
                    device_id_type=MESH,
                ).wait_recv()
                for to in range(4):
                    if to != plane:
                        onward(g, plane, to).start()

    def lead_begin(g):
        for plane in range(4):
            when(col != plane, lambda plane=plane: onward(g, plane, (plane + 1) % 4).wait_recv())
        lead_walk.begin(g)

    def onward_finish(g):
        for plane in range(4):
            @pl.when(col == plane)
            def _(plane=plane):
                for to in range(4):
                    if to != plane:
                        onward(g, plane, to).wait_send()

    def strip_copies(u):
        after, before = (col + 1) % 4, (col + 3) % 4

        def copy(src, dst, to, slot):
            return lambda: pltpu.make_async_remote_copy(
                src_ref=src,
                dst_ref=dst,
                send_sem=strip_send.at[u, slot],
                recv_sem=strip_recv.at[u, slot],
                device_id=(row, to),
                device_id_type=MESH,
            )

        low, high = pl.ds(0, B), pl.ds(B, B)
        near = [
            copy(strips.at[col, u, part], strips.at[col, u, part], to, slot)
            for slot, (part, to) in enumerate(((low, after), (high, before), (high, after), (low, before)))
        ]
        up, down = strips.at[before, u, low], strips.at[after, u, high]
        return near + [copy(up, up, after, 4), copy(down, down, before, 5)]

    def strip_begin(u):
        for entry in strip_copies(u)[:4]:
            entry().start()

    def strip_pass(u):
        sent = strip_copies(u)
        sent[0]().wait_recv()
        sent[4]().start()
        sent[1]().wait_recv()
        sent[5]().start()

    def strip_finish(u):
        sent = strip_copies(u)
        for i in range(2, 6):
            sent[i]().wait_recv()
        for entry in sent:
            entry().wait_send()

    def keep(u):
        return pltpu.make_async_copy(matrix_ref.at[:, pl.ds(u * B, B)], strips.at[col, u], keep_sem.at[u])

    def share_copy(n, e):
        to = base + e
        to_core, to_major, to_minor = place(to)
        return pltpu.make_async_remote_copy(
            src_ref=rounded_ref.at[pl.ds(e * share, share), lanes(n)],
            dst_ref=side_ref.at[to_core, to_major, to_minor, :, lanes(n)],
            send_sem=share_send.at[n, e],
            recv_sem=share_recv.at[n],
            device_id=(to, col),
            device_id_type=MESH,
        )

    def share_keep(n):
        return pltpu.make_async_copy(
            rounded_ref.at[pl.ds(pl.multiple_of(col * share, share), share), lanes(n)],
            side_ref.at[core, major, minor, :, lanes(n)],
            share_own,
        )

    def put_inverse(k, at_r, at_c, value):
        high, low = pieces(value)
        for start, part in ((0, high), (B, low), (2 * B, high)):
            inverse[k, at_r : at_r + H, start + at_c : start + at_c + H] = part

    def solve(n):
        acc[...] = strips[n % 4, n // 4]

        def update(j, carry):
            acc[...] -= dot_bf(rounded_ref[:, lanes(j)], lead[index_of(n, j)], NT)
            return carry

        lax.fori_loop(0, n, update, 0)
        solved = dot_inverse(acc[...], inverse[n])
        later = (at_row >= B) | (n < tile)
        rounded_ref[:, lanes(n)] = jnp.where(later, solved, 0.0).astype(BF16)

        @pl.when(n % 4 == col)
        def _():
            kept = later | ((n == tile) & (at_col <= at_row))
            panel_ref[n // 4] = jnp.where(kept, solved, 0.0)

        for e in range(4):
            when(is_source & (col != e), lambda e=e: share_copy(n, e).start())
        when(is_source, lambda: share_keep(n).start())

    def side_begin(n):
        when(is_source, lambda: share_keep(n).wait())
        when(jnp.logical_not(is_source), lambda: share_copy(n, (row + 1) % 4).wait_recv())
        side_walk.begin(n)

    def side_finish(n):
        side_walk.finish(n)
        for e in range(4):
            when(is_source & (col != e), lambda e=e: share_copy(n, e).wait_send())

    for u in range(2):
        keep(u).start()
    keep_nugget = pltpu.make_async_copy(nugget_hbm, nugget_ref, keep_sem.at[2])
    keep_nugget.start()

    partners = [(row_of(core, major, (minor + d) % 4), col) for d in (1, 2, 3)]
    partners += [(row_of(core, (major + d) % 4, minor), col) for d in (1, 2, 3)]
    partners += [(row + 1 - 2 * core, col)]
    partners += [(base + (row + d) % 4, col) for d in (1, 2, 3)]
    partners += [(row, (col + d) % 4) for d in (1, 2, 3)]
    barrier = pltpu.get_barrier_semaphore()
    for device in partners:
        pl.semaphore_signal(barrier, inc=1, device_id=device, device_id_type=MESH)
    for to in range(STEPS):
        @pl.when((col <= to) & (row != to))
        def _(to=to):
            pl.semaphore_signal(barrier, inc=1, device_id=(to, col), device_id_type=MESH)
    keep_nugget.wait()
    for u in range(2):
        keep(u).wait()

        @pl.when(col + 4 * u == row)
        def _(u=u):
            strips[col, u, 0:B] += jnp.where(at_row[0:B] == at_col[0:B], nugget_ref[:, 0:B], 0.0)

    owner = (row < STEPS) & (col <= row)
    pl.semaphore_wait(barrier, len(partners) + 31 * owner.astype(jnp.int32))

    each_fill(lambda entry: entry.start())
    for u in range(2):
        when(mine[u][2], lambda u=u: fill_own(u).start())
    onward_begin(0)
    strip_begin(0)
    lead_begin(0)
    onward_begin(1)
    lead_walk.second(0)
    lead_walk.third(0)
    lead_walk.fourth(0)
    lead_walk.finish(0)
    onward_finish(0)

    def step(k, carry):
        when(k == 4, lambda: lead_walk.finish(1))
        when(k == 4, lambda: onward_finish(1))
        at = tile_at(k, k)

        def row_tile(j, carry):
            here = tile_at(k, j)

            def update(i, carry):
                tiles[here] -= dot_bf(lead[index_of(k, i)], lead[index_of(j, i)], NT)
                return carry

            lax.fori_loop(0, j, update, 0)
            found = dot_inverse(tiles[here], inverse[j]).astype(BF16)
            lead[index_of(k, j)] = found
            tiles[at] -= dot_bf(found, found, NT)
            return carry

        lax.fori_loop(0, k, row_tile, 0)

        @pl.when(k == 1)
        def _():
            strip_finish(0)

        @pl.when(k == 5)
        def _():
            strip_finish(1)

        when(k >= 1, lambda: solve(k - 1))

        def half_step(h, carry):
            def at_half(value, condition, action):
                pl.when((h == value) & condition)(action)

            def early():
                at_half(0, k >= 3, lambda: side_walk.fourth(k - 3))
                at_half(0, k == 0, lambda: lead_begin(1))
                at_half(1, k >= 3, lambda: side_finish(k - 3))
                at_half(1, k >= 2, lambda: side_walk.third(k - 2))
                at_half(1, k == 0, lambda: lead_walk.second(1))

            def late():
                at_half(0, k >= 1, lambda: side_begin(k - 1))
                at_half(0, k == 0, lambda: strip_pass(0))
                at_half(1, k >= 1, lambda: side_walk.second(k - 1))

            @pl.when(h == 0)
            def _():
                diag[...] = tiles[at, 0:H, 0:H]

            done = inverse_factor([diag[8 * g : 8 * g + 8, :] for g in range(16)], {3: early, 11: late})
            for g in range(16):
                inv_half[8 * g : 8 * g + 8, :] = done[g]

            @pl.when(h == 0)
            def _():
                when(k == 1, lambda: lead_walk.third(1))
                when(k == 2, lambda: lead_walk.fourth(1))
                when(k == 1, lambda: strip_begin(1))
                when(k == 3, lambda: strip_pass(1))
                first = inv_half[...]
                l21 = dot_full(tiles[at, H:B, 0:H], first, NT)
                diag[...] = tiles[at, H:B, H:B] - dot_full(l21, l21, NT)
                mixed[...] = dot_full(l21, first, NN)
                put_inverse(k, 0, 0, first)
                put_inverse(k, 0, H, jnp.zeros((H, H), F32))

            @pl.when(h == 1)
            def _():
                second = inv_half[...]
                put_inverse(k, H, 0, -dot_full(second, mixed[...], NN))
                put_inverse(k, H, H, second)

            return carry

        return lax.fori_loop(0, 2, half_step, carry)

    lax.fori_loop(0, STEPS, step, 0)
    last = STEPS - 1
    solve(last)
    side_walk.fourth(last - 2)
    side_walk.third(last - 1)
    side_begin(last)
    side_finish(last - 2)
    side_walk.fourth(last - 1)
    side_walk.second(last)
    side_finish(last - 1)
    side_walk.third(last)
    side_walk.fourth(last)
    side_finish(last)
    each_fill(lambda entry: entry.wait_send())


def factor(matrix, nugget):
    vmem = pl.BlockSpec(memory_space=pltpu.VMEM)
    anywhere = pl.BlockSpec(memory_space=pltpu.HBM)
    dma = pltpu.SemaphoreType.DMA
    return pl.pallas_call(
        factor_kernel,
        out_shape=(
            jax.ShapeDtypeStruct((2, 2 * B, B), F32),
            jax.ShapeDtypeStruct((2 * B, STEPS * B), BF16),
            jax.ShapeDtypeStruct((2, 4, 4, H, STEPS * B), BF16),
        ),
        in_specs=[anywhere, anywhere],
        out_specs=(vmem, vmem, vmem),
        scratch_shapes=[
            pltpu.VMEM((1, 2 * B), F32),
            pltpu.VMEM((28, B, B), F32),
            pltpu.VMEM((4, 2, 2 * B, B), F32),
            pltpu.VMEM((28, B, B), BF16),
            pltpu.VMEM((STEPS, B, 3 * B), BF16),
            pltpu.VMEM((H, H), F32),
            pltpu.VMEM((H, H), F32),
            pltpu.VMEM((H, H), F32),
            pltpu.VMEM((2 * B, B), F32),
            dma((2, 32)), dma((2,)), dma((2, 4)), dma((2, 4)), dma((3,)), dma((STEPS, 4)), dma((STEPS,)), dma,
            dma((2, 6)), dma((2, 6)), dma((2, 13)), dma((2, 13)), dma((STEPS, 13)), dma((STEPS, 13)),
        ],
        compiler_params=pltpu.CompilerParams(
            has_side_effects=True, collective_id=0, vmem_limit_bytes=26 * 2**20
        ),
    )(matrix, nugget)


def trailing_kernel(matrix_ref, nugget_ref, panel_ref, rounded_ref, side_ref, out_ref):
    tile, col = lax.axis_index("row"), lax.axis_index("col")
    for u in range(WIDE):
        slot = pl.program_id(0) * WIDE + u
        col_tile = slot * 4 + col
        here = slice(u * B, (u + 1) * B)

        @pl.when(col_tile < STEPS)
        def _(slot=slot, here=here):
            out_ref[:, here] = panel_ref[jnp.minimum(slot, 1)]

        @pl.when(col_tile >= STEPS)
        def _(slot=slot, col_tile=col_tile, here=here):
            x, y = slot % 8 // 2, 2 * (slot % 2) + slot // 8
            side = jnp.concatenate([side_ref[0, x, y], side_ref[1, y, x]], axis=0)
            out_ref[:, here] = matrix_ref[:, here] - dot_bf(rounded_ref[...], side, NT)
            for s in range(2):
                @pl.when(col_tile == s * 32 + tile)
                def _(s=s):
                    rows = slice(s * B, (s + 1) * B)
                    at_row = lax.broadcasted_iota(jnp.int32, (B, B), 0)
                    at_col = lax.broadcasted_iota(jnp.int32, (B, B), 1)
                    out_ref[rows, here] += jnp.where(at_row == at_col, nugget_ref[:, rows], 0.0)

            @pl.when(tile < STEPS)
            def _():
                out_ref[0:B, here] = jnp.zeros((B, B), F32)


def trailing(matrix, nugget, panel, rounded, side):
    rows, cols = matrix.shape
    vmem = pl.BlockSpec(memory_space=pltpu.VMEM)
    return pl.pallas_call(
        trailing_kernel,
        grid=(cols // (WIDE * B),),
        out_shape=jax.ShapeDtypeStruct(matrix.shape, F32),
        in_specs=[
            pl.BlockSpec((rows, WIDE * B), lambda t: (0, t)),
            vmem, vmem, vmem, vmem,
        ],
        out_specs=pl.BlockSpec((rows, WIDE * B), lambda t: (0, t)),
        compiler_params=pltpu.CompilerParams(vmem_limit_bytes=20 * 2**20),
    )(matrix, nugget, panel, rounded, side)


def body(kernel, nugget):
    nugget = nugget.reshape(1, kernel.shape[0])
    panel, rounded, side = factor(pltpu.with_memory_space_constraint(kernel, pltpu.HBM), nugget)
    return trailing(kernel, nugget, panel, rounded, side)


def solution(mesh):
    return jax.shard_map(
        body,
        mesh=mesh,
        in_specs=(P("row", "col"), P("row")),
        out_specs=P("row", "col"),
        check_vma=False,
    )
```

```python
import jax
import jax.numpy as jnp
from jax import lax
from jax.experimental import pallas as pl
from jax.experimental.pallas import tpu as pltpu
from jax.sharding import PartitionSpec as P

B = 256
H = 128
STEPS = 7
WIDE = 2
F32 = jnp.float32
BF16 = jnp.bfloat16
MESH = pl.DeviceIdType.MESH
NT = (((1,), (1,)), ((), ()))
NN = (((1,), (0,)), ((), ()))


def pieces(x):
    high = x.astype(BF16)
    return high, (x - high.astype(F32)).astype(BF16)


def dot_full(a, b, dims):
    a_high, a_low = pieces(a)
    b_high, b_low = pieces(b)
    a_axis, b_axis = dims[0][0][0], dims[0][1][0]
    return dot_bf(
        jnp.concatenate([a_high, a_high, a_low], axis=a_axis),
        jnp.concatenate([b_high, b_low, b_high], axis=b_axis),
        dims,
    )


def dot_inverse(a, terms):
    high, low = pieces(a)
    return dot_bf(jnp.concatenate([high, high, low], axis=1), terms, NT)


def dot_bf(a, b, dims):
    return lax.dot_general(a, b, dims, preferred_element_type=F32)


def lane_splat(x, at):
    return jnp.broadcast_to(x[:, at : at + 1], x.shape)


def row_splat(x, at):
    return jnp.broadcast_to(x[at : at + 1, :], x.shape)


def inverse_factor(groups, hooks):
    lane = lax.broadcasted_iota(jnp.int32, (8, H), 1)
    sub = lax.broadcasted_iota(jnp.int32, (8, H), 0)
    groups = list(groups)
    result = []
    for b in range(16):
        if b in hooks:
            hooks[b]()
        start = 8 * b
        block = (lane >= start) & (lane < start + 8)
        here = groups[b]
        cols = [lane_splat(here, start + s) for s in range(8)]
        swept = jnp.where(block, jnp.where(lane - start == sub, 1.0, 0.0), here)
        scaled = pivots = jnp.ones((8, H), F32)
        for r in range(0, 8, 2):
            a, c, d = row_splat(cols[r], r), row_splat(cols[r + 1], r), row_splat(cols[r + 1], r + 1)
            det = a * d - c * c
            inv = 1.0 / det
            at_0, at_1 = sub == r, sub == r + 1
            inv_a = 1.0 / a

            def sweep(x):
                u, v = row_splat(x, r), row_splat(x, r + 1)
                first, second = (d * u - c * v) * inv, (a * v - c * u) * inv
                rest = x - (cols[r] * first + cols[r + 1] * second)
                return jnp.where(at_0, first, jnp.where(at_1, second, rest)), u, v

            new, u, v = sweep(swept)
            scaled = jnp.where(at_0, u, jnp.where(at_1, v - (c * inv_a) * u, scaled))
            pivots = jnp.where(at_0, a, jnp.where(at_1, det * inv_a, pivots))
            swept = new
            for j in range(r + 2, 8):
                cols[j] = sweep(cols[j])[0]
        result.append(jnp.where(lane <= sub + start, scaled * lax.rsqrt(pivots), 0.0))
        rows = [row_splat(swept, s) for s in range(8)]
        near = min(b + 1, 15)
        if near < 15:
            zero = jnp.zeros((8, H), F32)
            spread = jnp.concatenate([swept if g == b else zero for g in range(16)], axis=0)
            far = dot_full(jnp.concatenate(groups[near + 1 :], axis=0), spread, NN)
        for g in range(b + 1, near + 1):
            terms = [lane_splat(groups[g], start + s) * rows[s] for s in range(8)]
            while len(terms) > 1:
                terms = [terms[i] + terms[i + 1] for i in range(0, len(terms), 2)]
            groups[g] = jnp.where(block, 0.0, groups[g]) - terms[0]
        for g in range(near + 1, 16):
            at = 8 * (g - near - 1)
            groups[g] = jnp.where(block, 0.0, groups[g]) - far[at : at + 8]
    return result


def place(row):
    core, y, x = row % 2, row // 2 % 4, row // 8
    return core, x * (1 - core) + y * core, y * (1 - core) + x * core


def row_of(core, major, minor):
    x = major * (1 - core) + minor * core
    y = minor * (1 - core) + major * core
    return (x * 4 + y) * 2 + core


class Walk:
    def __init__(self, single, low, high, whole, send, recv, direct=False):
        self.row, self.col = lax.axis_index("row"), lax.axis_index("col")
        self.core, self.major, self.minor = place(self.row)
        self.parts = single, low, high, whole
        self.send, self.recv, self.direct = send, recv, direct

    def copies(self, n):
        single, low, high, whole = self.parts
        core, major, minor = self.core, self.major, self.minor

        def copy(ref, device, slot):
            return lambda: pltpu.make_async_remote_copy(
                src_ref=ref,
                dst_ref=ref,
                send_sem=self.send.at[n, slot],
                recv_sem=self.recv.at[n, slot],
                device_id=(device, self.col),
                device_id_type=MESH,
            )

        first = [
            copy(single(n, minor), row_of(core, major, (minor + d) % 4), i) for i, d in enumerate((1, 3, 2))
        ]
        after, before = (major + 1) % 4, (major + 3) % 4
        up, down = row_of(core, after, minor), row_of(core, before, minor)
        second = [
            copy(low(n, major), up, 3),
            copy(high(n, major), down, 4),
            copy(high(n, major), up, 5),
            copy(low(n, major), down, 6),
            copy(low(n, before), up, 7),
            copy(high(n, after), down, 8),
        ]
        if self.direct:
            block = whole(n, major)
            second = [copy(block, row_of(core, (major + d) % 4, minor), 3 + i) for i, d in enumerate((1, 3, 2))]
        sibling = self.row + 1 - 2 * core
        order = (major, before, after, (major + 2) % 4)
        start = 3 + len(second)
        return first + second + [copy(whole(n, at), sibling, start + i) for i, at in enumerate(order)]

    def begin(self, n):
        sent = self.copies(n)
        for i in (2, 0, 1):
            sent[i]().start()

    def second(self, n):
        sent = self.copies(n)
        for i in range(3):
            sent[i]().wait_recv()
        for i in (5, 3, 4, 6) if self.direct else (3, 4, 5, 6, 9):
            sent[i]().start()

    def third(self, n):
        sent = self.copies(n)
        if self.direct:
            for i in range(3, 6):
                sent[i]().wait_recv()
                sent[i + 4]().start()
            return
        sent[3]().wait_recv()
        sent[7]().start()
        sent[4]().wait_recv()
        sent[8]().start()
        sent[5]().wait_recv()
        sent[10]().start()
        sent[6]().wait_recv()
        sent[11]().start()

    def fourth(self, n):
        sent = self.copies(n)
        sent[7]().wait_recv()
        sent[8]().wait_recv()
        sent[12]().start()

    def finish(self, n):
        sent = self.copies(n)
        for entry in sent[-4:]:
            entry().wait_recv()
        for entry in sent:
            entry().wait_send()


GROUP_START = (0, 10)
GROUP_SIZE = (10, 18)
FROM_PLANE = ((4, 3, 2, 1), (6, 5, 4, 3))


def from_plane_start(group, plane):
    return GROUP_START[group] + sum(FROM_PLANE[group][:plane])


def tile_at(i, j):
    plane = j % 4
    early = 4 * j - j * (j - 1) // 2 + i - j
    late = 10 + 6 * plane - plane * (plane - 1) // 2 + jnp.where(j < 4, i - 4, 3 + i - j)
    return jnp.where(i < 4, early, late)


def index_of(i, j):
    return i * (i + 1) // 2 + j


def lanes(k):
    return pl.ds(pl.multiple_of(k * B, B), B)


def factor_kernel(
    matrix_ref, nugget_hbm, panel_ref, rounded_ref, side_ref,
    nugget_ref, tiles, strips, lead, inverse, diag, inv_half, mixed, acc,
    fill_send, fill_recv, onward_send, onward_recv, keep_sem, share_send, share_recv, share_own,
    strip_send, strip_recv, lead_send, lead_recv, side_send, side_recv,
):
    row, col = lax.axis_index("row"), lax.axis_index("col")
    core, major, minor = place(row)
    tile = row
    base = row // 4 * 4
    is_source = row % 4 == col
    share = rounded_ref.shape[0] // 4
    at_row = lax.broadcasted_iota(jnp.int32, (2 * B, B), 0)
    at_col = lax.broadcasted_iota(jnp.int32, (2 * B, B), 1)

    def when(condition, action):
        @pl.when(condition)
        def _():
            action()

    def span(start, size):
        return pl.ds(pl.multiple_of(start, 8), size)

    def group_tiles(g):
        return pl.ds(GROUP_START[g], GROUP_SIZE[g])

    lead_walk = Walk(
        lambda g, at: tiles.at[group_tiles(g), span(8 * (core * 16 + major * 4 + at), 8)],
        lambda g, at: tiles.at[group_tiles(g), span(8 * (core * 16 + at * 4), 16)],
        lambda g, at: tiles.at[group_tiles(g), span(8 * (core * 16 + at * 4) + 16, 16)],
        lambda g, at: tiles.at[group_tiles(g), span(8 * (core * 16 + at * 4), 32)],
        lead_send,
        lead_recv,
    )
    half = 2
    side_walk = Walk(
        lambda n, at: side_ref.at[core, major, at, :, lanes(n)],
        lambda n, at: side_ref.at[core, at, pl.ds(0, half), :, lanes(n)],
        lambda n, at: side_ref.at[core, at, pl.ds(half, half), :, lanes(n)],
        lambda n, at: side_ref.at[core, at, :, :, lanes(n)],
        side_send,
        side_recv,
    )

    piece = span(8 * (core * 16 + major * 4 + minor), 8)
    mine = []
    for u in range(2):
        mine.append((tile_at(row, col + 4 * u), (row >= 4).astype(jnp.int32), (row < STEPS) & (col + 4 * u <= row)))

    def fill(u, to):
        to_core, to_major, to_minor = place(to)
        there = span(8 * (to_core * 16 + to_major * 4 + to_minor), 8)
        return pltpu.make_async_remote_copy(
            src_ref=strips.at[col, u, there],
            dst_ref=tiles.at[mine[u][0], there],
            send_sem=fill_send.at[u, to],
            recv_sem=fill_recv.at[mine[u][1]],
            device_id=(to, col),
            device_id_type=MESH,
        )

    def fill_own(u):
        return pltpu.make_async_copy(
            strips.at[col, u, piece], tiles.at[mine[u][0], piece], fill_recv.at[mine[u][1]]
        )

    def each_fill(action):
        def one(to, carry):
            for u in range(2):
                when((to != row) & mine[u][2], lambda u=u: action(fill(u, to)))
            return carry

        when(row < STEPS, lambda: lax.fori_loop(0, 32, one, 0))

    def onward(g, plane, to):
        block = tiles.at[pl.ds(from_plane_start(g, plane), FROM_PLANE[g][plane]), piece]
        return pltpu.make_async_remote_copy(
            src_ref=block,
            dst_ref=block,
            send_sem=onward_send.at[g, to],
            recv_sem=onward_recv.at[g, plane],
            device_id=(row, to),
            device_id_type=MESH,
        )

    def onward_begin(g):
        for plane in range(4):
            @pl.when(col == plane)
            def _(plane=plane):
                block = tiles.at[pl.ds(from_plane_start(g, plane), FROM_PLANE[g][plane]), piece]
                pltpu.make_async_remote_copy(
                    src_ref=block,
                    dst_ref=block,
                    send_sem=onward_send.at[g, plane],
                    recv_sem=fill_recv.at[g],
                    device_id=(base + (row + 1) % 4, col),
                    device_id_type=MESH,
                ).wait_recv()
                for to in range(4):
                    if to != plane:
                        onward(g, plane, to).start()

    def lead_begin(g):
        for plane in range(4):
            when(col != plane, lambda plane=plane: onward(g, plane, (plane + 1) % 4).wait_recv())
        lead_walk.begin(g)

    def onward_finish(g):
        for plane in range(4):
            @pl.when(col == plane)
            def _(plane=plane):
                for to in range(4):
                    if to != plane:
                        onward(g, plane, to).wait_send()

    def strip_copies(u):
        after, before = (col + 1) % 4, (col + 3) % 4

        def copy(src, dst, to, slot):
            return lambda: pltpu.make_async_remote_copy(
                src_ref=src,
                dst_ref=dst,
                send_sem=strip_send.at[u, slot],
                recv_sem=strip_recv.at[u, slot],
                device_id=(row, to),
                device_id_type=MESH,
            )

        low, high = pl.ds(0, B), pl.ds(B, B)
        near = [
            copy(strips.at[col, u, part], strips.at[col, u, part], to, slot)
            for slot, (part, to) in enumerate(((low, after), (high, before), (high, after), (low, before)))
        ]
        up, down = strips.at[before, u, low], strips.at[after, u, high]
        return near + [copy(up, up, after, 4), copy(down, down, before, 5)]

    def strip_begin(u):
        for entry in strip_copies(u)[:4]:
            entry().start()

    def strip_pass(u):
        sent = strip_copies(u)
        sent[0]().wait_recv()
        sent[4]().start()
        sent[1]().wait_recv()
        sent[5]().start()

    def strip_finish(u):
        sent = strip_copies(u)
        for i in range(2, 6):
            sent[i]().wait_recv()
        for entry in sent:
            entry().wait_send()

    def keep(u):
        return pltpu.make_async_copy(matrix_ref.at[:, pl.ds(u * B, B)], strips.at[col, u], keep_sem.at[u])

    def share_copy(n, e):
        to = base + e
        to_core, to_major, to_minor = place(to)
        return pltpu.make_async_remote_copy(
            src_ref=rounded_ref.at[pl.ds(e * share, share), lanes(n)],
            dst_ref=side_ref.at[to_core, to_major, to_minor, :, lanes(n)],
            send_sem=share_send.at[n, e],
            recv_sem=share_recv.at[n],
            device_id=(to, col),
            device_id_type=MESH,
        )

    def share_keep(n):
        return pltpu.make_async_copy(
            rounded_ref.at[pl.ds(pl.multiple_of(col * share, share), share), lanes(n)],
            side_ref.at[core, major, minor, :, lanes(n)],
            share_own,
        )

    def put_inverse(k, at_r, at_c, value):
        high, low = pieces(value)
        for start, part in ((0, high), (B, low), (2 * B, high)):
            inverse[k, at_r : at_r + H, start + at_c : start + at_c + H] = part

    def solve(n):
        acc[...] = strips[n % 4, n // 4]

        def update(j, carry):
            acc[...] -= dot_bf(rounded_ref[:, lanes(j)], lead[index_of(n, j)], NT)
            return carry

        lax.fori_loop(0, n, update, 0)
        solved = dot_inverse(acc[...], inverse[n])
        later = (at_row >= B) | (n < tile)
        rounded_ref[:, lanes(n)] = jnp.where(later, solved, 0.0).astype(BF16)

        @pl.when(n % 4 == col)
        def _():
            kept = later | ((n == tile) & (at_col <= at_row))
            panel_ref[n // 4] = jnp.where(kept, solved, 0.0)

        for e in range(4):
            when(is_source & (col != e), lambda e=e: share_copy(n, e).start())
        when(is_source, lambda: share_keep(n).start())

    def side_begin(n):
        when(is_source, lambda: share_keep(n).wait())
        when(jnp.logical_not(is_source), lambda: share_copy(n, (row + 1) % 4).wait_recv())
        side_walk.begin(n)

    def side_finish(n):
        side_walk.finish(n)
        for e in range(4):
            when(is_source & (col != e), lambda e=e: share_copy(n, e).wait_send())

    for u in range(2):
        keep(u).start()
    keep_nugget = pltpu.make_async_copy(nugget_hbm, nugget_ref, keep_sem.at[2])
    keep_nugget.start()

    partners = [(row_of(core, major, (minor + d) % 4), col) for d in (1, 2, 3)]
    partners += [(row_of(core, (major + d) % 4, minor), col) for d in (1, 2, 3)]
    partners += [(row + 1 - 2 * core, col)]
    partners += [(base + (row + d) % 4, col) for d in (1, 2, 3)]
    partners += [(row, (col + d) % 4) for d in (1, 2, 3)]
    barrier = pltpu.get_barrier_semaphore()
    for device in partners:
        pl.semaphore_signal(barrier, inc=1, device_id=device, device_id_type=MESH)
    for to in range(STEPS):
        @pl.when((col <= to) & (row != to))
        def _(to=to):
            pl.semaphore_signal(barrier, inc=1, device_id=(to, col), device_id_type=MESH)
    keep_nugget.wait()
    for u in range(2):
        keep(u).wait()

        @pl.when(col + 4 * u == row)
        def _(u=u):
            strips[col, u, 0:B] += jnp.where(at_row[0:B] == at_col[0:B], nugget_ref[:, 0:B], 0.0)

    owner = (row < STEPS) & (col <= row)
    pl.semaphore_wait(barrier, len(partners) + 31 * owner.astype(jnp.int32))

    each_fill(lambda entry: entry.start())
    for u in range(2):
        when(mine[u][2], lambda u=u: fill_own(u).start())
    onward_begin(0)
    lead_begin(0)
    lead_walk.second(0)
    onward_begin(1)
    strip_begin(0)
    lead_walk.third(0)
    lead_walk.fourth(0)
    lead_walk.finish(0)
    onward_finish(0)

    def step(k, carry):
        when(k == 4, lambda: lead_walk.finish(1))
        when(k == 4, lambda: onward_finish(1))
        at = tile_at(k, k)

        def row_tile(j, carry):
            here = tile_at(k, j)

            def update(i, carry):
                tiles[here] -= dot_bf(lead[index_of(k, i)], lead[index_of(j, i)], NT)
                return carry

            lax.fori_loop(0, j, update, 0)
            found = dot_inverse(tiles[here], inverse[j]).astype(BF16)
            lead[index_of(k, j)] = found
            tiles[at] -= dot_bf(found, found, NT)
            return carry

        lax.fori_loop(0, k, row_tile, 0)

        @pl.when(k == 1)
        def _():
            strip_finish(0)

        @pl.when(k == 5)
        def _():
            strip_finish(1)

        when(k >= 1, lambda: solve(k - 1))

        def half_step(h, carry):
            def at_half(value, condition, action):
                pl.when((h == value) & condition)(action)

            def early():
                at_half(0, k >= 3, lambda: side_walk.fourth(k - 3))
                at_half(0, k == 0, lambda: lead_begin(1))
                at_half(1, k >= 3, lambda: side_finish(k - 3))
                at_half(1, k >= 2, lambda: side_walk.third(k - 2))
                at_half(1, k == 0, lambda: lead_walk.second(1))

            def late():
                at_half(0, k >= 1, lambda: side_begin(k - 1))
                at_half(0, k == 0, lambda: strip_pass(0))
                at_half(1, k >= 1, lambda: side_walk.second(k - 1))

            @pl.when(h == 0)
            def _():
                diag[...] = tiles[at, 0:H, 0:H]

            done = inverse_factor([diag[8 * g : 8 * g + 8, :] for g in range(16)], {3: early, 11: late})
            for g in range(16):
                inv_half[8 * g : 8 * g + 8, :] = done[g]

            @pl.when(h == 0)
            def _():
                when(k == 1, lambda: lead_walk.third(1))
                when(k == 2, lambda: lead_walk.fourth(1))
                when(k == 1, lambda: strip_begin(1))
                when(k == 3, lambda: strip_pass(1))
                first = inv_half[...]
                l21 = dot_full(tiles[at, H:B, 0:H], first, NT)
                diag[...] = tiles[at, H:B, H:B] - dot_full(l21, l21, NT)
                mixed[...] = dot_full(l21, first, NN)
                put_inverse(k, 0, 0, first)
                put_inverse(k, 0, H, jnp.zeros((H, H), F32))

            @pl.when(h == 1)
            def _():
                second = inv_half[...]
                put_inverse(k, H, 0, -dot_full(second, mixed[...], NN))
                put_inverse(k, H, H, second)

            return carry

        return lax.fori_loop(0, 2, half_step, carry)

    lax.fori_loop(0, STEPS, step, 0)
    last = STEPS - 1
    solve(last)
    side_walk.fourth(last - 2)
    side_walk.third(last - 1)
    side_begin(last)
    side_finish(last - 2)
    side_walk.fourth(last - 1)
    side_walk.second(last)
    side_finish(last - 1)
    side_walk.third(last)
    side_walk.fourth(last)
    side_finish(last)
    each_fill(lambda entry: entry.wait_send())


def factor(matrix, nugget):
    vmem = pl.BlockSpec(memory_space=pltpu.VMEM)
    anywhere = pl.BlockSpec(memory_space=pltpu.HBM)
    dma = pltpu.SemaphoreType.DMA
    return pl.pallas_call(
        factor_kernel,
        out_shape=(
            jax.ShapeDtypeStruct((2, 2 * B, B), F32),
            jax.ShapeDtypeStruct((2 * B, STEPS * B), BF16),
            jax.ShapeDtypeStruct((2, 4, 4, H, STEPS * B), BF16),
        ),
        in_specs=[anywhere, anywhere],
        out_specs=(vmem, vmem, vmem),
        scratch_shapes=[
            pltpu.VMEM((1, 2 * B), F32),
            pltpu.VMEM((28, B, B), F32),
            pltpu.VMEM((4, 2, 2 * B, B), F32),
            pltpu.VMEM((28, B, B), BF16),
            pltpu.VMEM((STEPS, B, 3 * B), BF16),
            pltpu.VMEM((H, H), F32),
            pltpu.VMEM((H, H), F32),
            pltpu.VMEM((H, H), F32),
            pltpu.VMEM((2 * B, B), F32),
            dma((2, 32)), dma((2,)), dma((2, 4)), dma((2, 4)), dma((3,)), dma((STEPS, 4)), dma((STEPS,)), dma,
            dma((2, 6)), dma((2, 6)), dma((2, 13)), dma((2, 13)), dma((STEPS, 13)), dma((STEPS, 13)),
        ],
        compiler_params=pltpu.CompilerParams(
            has_side_effects=True, collective_id=0, vmem_limit_bytes=26 * 2**20
        ),
    )(matrix, nugget)


def trailing_kernel(matrix_ref, nugget_ref, panel_ref, rounded_ref, side_ref, out_ref):
    tile, col = lax.axis_index("row"), lax.axis_index("col")
    for u in range(WIDE):
        slot = pl.program_id(0) * WIDE + u
        col_tile = slot * 4 + col
        here = slice(u * B, (u + 1) * B)

        @pl.when(col_tile < STEPS)
        def _(slot=slot, here=here):
            out_ref[:, here] = panel_ref[jnp.minimum(slot, 1)]

        @pl.when(col_tile >= STEPS)
        def _(slot=slot, col_tile=col_tile, here=here):
            x, y = slot % 8 // 2, 2 * (slot % 2) + slot // 8
            side = jnp.concatenate([side_ref[0, x, y], side_ref[1, y, x]], axis=0)
            out_ref[:, here] = matrix_ref[:, here] - dot_bf(rounded_ref[...], side, NT)
            for s in range(2):
                @pl.when(col_tile == s * 32 + tile)
                def _(s=s):
                    rows = slice(s * B, (s + 1) * B)
                    at_row = lax.broadcasted_iota(jnp.int32, (B, B), 0)
                    at_col = lax.broadcasted_iota(jnp.int32, (B, B), 1)
                    out_ref[rows, here] += jnp.where(at_row == at_col, nugget_ref[:, rows], 0.0)

            @pl.when(tile < STEPS)
            def _():
                out_ref[0:B, here] = jnp.zeros((B, B), F32)


def trailing(matrix, nugget, panel, rounded, side):
    rows, cols = matrix.shape
    vmem = pl.BlockSpec(memory_space=pltpu.VMEM)
    return pl.pallas_call(
        trailing_kernel,
        grid=(cols // (WIDE * B),),
        out_shape=jax.ShapeDtypeStruct(matrix.shape, F32),
        in_specs=[
            pl.BlockSpec((rows, WIDE * B), lambda t: (0, t)),
            vmem, vmem, vmem, vmem,
        ],
        out_specs=pl.BlockSpec((rows, WIDE * B), lambda t: (0, t)),
        compiler_params=pltpu.CompilerParams(vmem_limit_bytes=20 * 2**20),
    )(matrix, nugget, panel, rounded, side)


def body(kernel, nugget):
    nugget = nugget.reshape(1, kernel.shape[0])
    panel, rounded, side = factor(pltpu.with_memory_space_constraint(kernel, pltpu.HBM), nugget)
    return trailing(kernel, nugget, panel, rounded, side)


def solution(mesh):
    return jax.shard_map(
        body,
        mesh=mesh,
        in_specs=(P("row", "col"), P("row")),
        out_specs=P("row", "col"),
        check_vma=False,
    )
```
